32 devices in a mesh: row: 16 (over z, y, core), rep: 2 (over x).
Axes of the slice: x: 2, y: 2, z: 4, core: 2. Of those that a mesh axis runs over, the one named last changes fastest.
Arguments:
- features: bfloat16 [8192, 128], P('row'), may hold values from -6 to 6
- input_weight: bfloat16 [128, 512], replicated, may hold values from -5 to 5
- output_weight: bfloat16 [512, 512], replicated, may hold values from -0.25 to 0.25
- cotangent: bfloat16 [8192, 512], P(('row', 'rep')), may hold values from -0.25 to 0.25
- adjacency_tiles: bfloat16 [64, 8, 128, 128], P('row', 'rep'), may hold values from 0.0009994507 to 1
- block_columns: int32 [64, 8], P('row', 'rep'), may hold values from 0 to 63, as said below
- graph_sizes: int32 [16], replicated, may hold values from 1 to 2048, 8192 in all
Outputs:
- scores: bfloat16 [8192, 512], P(('row', 'rep'))
- grad_input: float32 [128, 512], replicated
- grad_output: float32 [512, 512], replicated
The draws below stay inside these ranges and needn't reach their ends.
Inputs may be any that keep to these rules, and one draw needn't show every extreme that they name: `block_columns`: each row block b lists 8 distinct column blocks, its own first, every one within 12 blocks of b along the closed loop of 64 blocks (indices taken mod 64); row block 0 lists the blocks at both ends of that reach. `graph_sizes`: the sizes sum to 8192.
All inputs are finite; a program needn't handle non-finite values.
Results may differ from the reference program's by a relative error of at most 0.0045.
The reference program's roundings to bfloat16 on the way (of `masked`, `first`, `hidden`, `second`, `scaled` and `delta`) count: a program that leaves them out, or rounds other values in their place, can miss the bound.
Values may be sent and summed in bfloat16 or wider, within the bound.
A program may use at most 64 MiB of HBM per device.

```python
import math
import jax
import jax.numpy as jnp
import numpy as np
from jax import lax

TILE = 128
F_IN = 128
HID = 512
RB = 4
HOPS = 3
KT = 8
NBLK = 64
NODES = 8192
GRAPHS = 16


def draw_block_columns(key, part):
    reach = HOPS * RB
    offsets = jnp.concatenate([jnp.arange(-reach, 0), jnp.arange(1, reach + 1)]).astype(jnp.int32)
    raw = jax.random.randint(key, (NBLK, 2 * reach), 0, 2 ** 20)
    scores = raw * (2 * reach) + jnp.arange(2 * reach, dtype=jnp.int32)[None, :]
    forced = (jnp.arange(NBLK)[:, None] == 0) & (jnp.abs(offsets)[None, :] == reach)
    scores = jnp.where(forced, jnp.arange(2 * reach, dtype=jnp.int32)[None, :] - 4 * reach, scores)
    order = jnp.argsort(scores, axis=1)[:, :KT - 1]
    chosen = offsets[order]
    shifts = jnp.concatenate([jnp.zeros((NBLK, 1), jnp.int32), chosen], axis=1)
    return ((jnp.arange(NBLK, dtype=jnp.int32)[:, None] + shifts) % NBLK).astype(jnp.int32)


def raised(values, stream_key, source, target, blocks, factor):
    owner, partner = [(jnp.arange(values.shape[position]) // (values.shape[position] // blocks)).reshape([-1 if axis == position else 1 for axis in range(values.ndim)]) for position in (source, target)]
    chosen = jax.random.permutation(stream_key, blocks)[partner]
    strong = (owner == chosen) | (owner == (partner + blocks // 2) % blocks)
    return jnp.where(strong, factor * values, values)


def block_levels(stream_key, extent, cuts, least, largest):
    gain = 1.0
    for dim, parts in cuts:
        heights = jax.random.uniform(jax.random.fold_in(jax.random.fold_in(stream_key, 6), dim), (parts,), jnp.float32, least / len(cuts), largest / len(cuts))
        gain = gain * jnp.repeat(jnp.exp(heights), extent[dim] // parts).reshape((-1,) + (1,) * (len(extent) - 1 - dim))
    return gain


def profile(count, total, limit, skew):
    weights = [(1 << 20) // math.isqrt(standing ** skew) + 1 for standing in range(2, count + 1)]
    surplus, holding = total - limit - (count - 1), [1] * (count - 1)
    while surplus > 0:
        movable = [i for i in range(count - 1) if holding[i] < limit]
        mass, remaining = sum([weights[i] for i in movable]), surplus
        for i in movable:
            addition = min(limit - holding[i], max(1, remaining * weights[i] // mass), surplus)
            holding[i] = holding[i] + addition
            surplus = surplus - addition
    return np.array([limit] + holding)


def uneven(stream_key, number_of, total, most, slope):
    if number_of == 2:
        one = jax.random.randint(stream_key, (), max(1, total - most), min(most, total - 1) + 1)
        return jnp.stack([one, total - one])
    lengths = jnp.asarray(profile(number_of, total, most, slope), jnp.int32)
    twos = (number_of - 1) // 2
    donor, receiver = lengths[1:1 + 2 * twos:2], lengths[2:2 + 2 * twos:2]
    room = jnp.minimum(donor - 1, most - receiver)
    shifted = jax.random.randint(jax.random.fold_in(stream_key, 1), (twos,), 0, 1 << 20) % (room + 1)
    lengths = lengths.at[1:1 + 2 * twos:2].set(donor - shifted).at[2:2 + 2 * twos:2].set(receiver + shifted)
    return lengths[jax.random.permutation(jax.random.fold_in(stream_key, 2), number_of)]


def noise(rng, extent, scale, limit, shards=(), kind=jnp.bfloat16):
    entries = scale * jax.random.normal(rng, extent, jnp.float32)
    if shards:
        entries = entries * block_levels(rng, extent, shards, -0.22, 0.18)
    return jnp.clip(entries, -limit, limit).astype(kind)


def bell_draw_with(own_key, dims, spread, bound, split, heavy, kind=jnp.bfloat16):
    result = spread * jax.random.normal(own_key, dims, jnp.float32)
    if split:
        result = result * block_levels(own_key, dims, split, -0.22, 0.18)
    return jnp.clip(raised(result, jax.random.fold_in(own_key, 3), *heavy), -bound, bound).astype(kind)


def setup_inputs(seed: int = 0) -> dict:
    arg_keys = jax.random.split(jax.random.key(seed), 8)
    return {
        "features": noise(arg_keys[0], (NODES, F_IN), 1.0, 6.0, ((0, 16),)),
        "input_weight": noise(arg_keys[1], (F_IN, HID), 1.0, 5.0),
        "output_weight": noise(arg_keys[2], (HID, HID), HID ** -0.5, 0.25),
        "cotangent": bell_draw_with(arg_keys[3], (NODES, HID), 0.01, 0.25, ((0, 32),), (0, 1, 32, 2.75)),
        "adjacency_tiles": jnp.clip(jnp.exp(math.log(1.0) - 6.9083047 * jax.random.uniform(arg_keys[4], (NBLK, KT, TILE, TILE), jnp.float32) ** block_levels(arg_keys[4], (NBLK, KT, TILE, TILE), ((0, 16), (1, 2)), -0.2, 0.2)), 0.0009994507, 1.0).astype(jnp.bfloat16),
        "block_columns": draw_block_columns(jax.random.fold_in(arg_keys[7], 71), 0),
        "graph_sizes": uneven(arg_keys[6], GRAPHS, NODES, 16 * TILE, 2).astype(jnp.int32),
    }


def graph_of(nodes, ends):
    return lax.optimization_barrier(jnp.sum((nodes[..., None] >= ends).astype(jnp.int32), axis=-1))

def reference(features, input_weight, output_weight, cotangent, adjacency_tiles, block_columns, graph_sizes):
    ends = jnp.cumsum(graph_sizes).astype(jnp.int32)
    blocks = adjacency_tiles.shape[0]
    tile = adjacency_tiles.shape[2]
    within = jnp.arange(tile, dtype=jnp.int32)
    row_ids = graph_of(jnp.arange(blocks, dtype=jnp.int32)[:, None] * tile + within, ends)
    col_ids = graph_of(block_columns[..., None] * tile + within, ends)
    same = row_ids[:, None, :, None] == col_ids[:, :, None, :]
    masked = jnp.where(same, adjacency_tiles, jnp.zeros_like(adjacency_tiles))
    degree = 1.0 + lax.optimization_barrier(jnp.sum(masked.astype(jnp.float32), axis=(1, 3))).reshape(-1)

    def aggregate(values):
        grid = values.reshape(blocks, tile, -1)

        def single(pair):
            tiles_here, columns_here = pair
            return jnp.einsum('kij,kjf->if', tiles_here.astype(jnp.float32), grid[columns_here], precision=lax.Precision.HIGHEST)
        return lax.map(single, (masked, block_columns)).reshape(blocks * tile, -1)
    feats = features.astype(jnp.float32)
    first = ((aggregate(feats) + feats) / degree[:, None]).astype(jnp.bfloat16)
    preact = jnp.dot(first, input_weight, preferred_element_type=jnp.float32)
    hidden = jnp.maximum(preact, 0.0).astype(jnp.bfloat16)
    hidden_wide = hidden.astype(jnp.float32)
    second = ((aggregate(hidden_wide) + hidden_wide) / degree[:, None]).astype(jnp.bfloat16)
    scores = jnp.dot(second, output_weight, preferred_element_type=jnp.float32).astype(jnp.bfloat16)
    grad_output = jnp.dot(second.T, cotangent, preferred_element_type=jnp.float32)
    scaled = (jnp.dot(cotangent, output_weight.T, preferred_element_type=jnp.float32) / degree[:, None]).astype(jnp.bfloat16)
    unused, pullback = jax.vjp(aggregate, hidden_wide)
    transposed, = pullback(scaled.astype(jnp.float32))
    back = transposed + scaled.astype(jnp.float32)
    delta = jnp.where(preact > 0.0, back, 0.0).astype(jnp.bfloat16)
    grad_input = jnp.dot(first.T, delta, preferred_element_type=jnp.float32)
    return (scores, grad_input, grad_output)
```

```python
import functools

import jax
import jax.numpy as jnp
from jax import lax
from jax.experimental import pallas as pl
from jax.experimental.pallas import tpu as pltpu
from jax.sharding import PartitionSpec as P

HOPS = 3
SPAN = 2 * HOPS + 1
MESH = pl.DeviceIdType.MESH
ANY = pl.BlockSpec(memory_space=pl.ANY)
HBM = pl.BlockSpec(memory_space=pltpu.HBM)
VMEM = pl.BlockSpec(memory_space=pltpu.VMEM)
SMEM = pl.BlockSpec(memory_space=pltpu.SMEM)
F32 = jnp.float32
BF16 = jnp.bfloat16


def dot(a, b, dims):
    return lax.dot_general(a, b, ((dims[:1], dims[1:]), ((), ())), preferred_element_type=F32)


def greet(peers):
    barrier = pltpu.get_barrier_semaphore()
    for peer in peers:
        pl.semaphore_signal(barrier, inc=1, device_id=peer, device_id_type=MESH)
    pl.semaphore_wait(barrier, len(peers))


def remote(src, dst, send, recv, index, peer):
    return pltpu.make_async_remote_copy(
        src_ref=src, dst_ref=dst, send_sem=send.at[index], recv_sem=recv.at[index],
        device_id=peer, device_id_type=MESH,
    )


def places(rows):
    row, rep = lax.axis_index("row"), lax.axis_index("rep")
    core = lax.rem(row, 2)
    flip, far = 1 - 2 * core, 6 * core - 3

    def at(shift):
        return (lax.rem(row + shift + rows, rows), rep)

    return flip, far, at


def start_rows(rows, src, band, send, recv, base):
    flip, far, at = places(rows)
    copies = [remote(src, band.at[HOPS - shift], send, recv, base + n, at(shift))
              for n, shift in enumerate((2, -2, far, flip))]
    for copy in copies:
        copy.start()
    return copies


def finish_rows(rows, copies, band, send, recv, base):
    flip, far, at = places(rows)
    passed = []
    for n, shift in enumerate((2, -2)):
        copies[n].wait_recv()
        step = remote(band.at[HOPS - shift], band.at[HOPS - shift - flip], send, recv, base + n, at(flip))
        step.start()
        passed.append(step)
    for copy in copies[2:]:
        copy.wait_recv()
    for copy in copies:
        copy.wait_send()
    for copy in passed:
        copy.wait()


def open_kernel(rows, reps, feats, cot, tiles, cols, band, cots, all_tiles, all_cols, send, recv, local):
    row, rep = lax.axis_index("row"), lax.axis_index("rep")
    flip, far, at = places(rows)
    others = [(row, lax.rem(rep + t, reps)) for t in range(1, reps)]
    greet([at(2), at(-2), at(far), at(flip)] + others)
    copies, n = [], 0
    pieces = ((tiles, all_tiles), (cols, all_cols), (cot, cots))
    pieces = pieces if cot is not None else pieces[:2]
    for peer in others:
        for src, dst in pieces:
            copies.append(remote(src, dst.at[rep], send, recv, n, peer))
            n += 1
    for i, (src, dst) in enumerate(pieces):
        copies.append(pltpu.make_async_copy(src, dst.at[rep], local.at[i]))
    copies.append(pltpu.make_async_copy(feats, band.at[HOPS], local.at[3]))
    for copy in copies:
        copy.start()
    moved = start_rows(rows, feats, band, send, recv, n)
    finish_rows(rows, moved, band, send, recv, n + 4)
    for copy in copies:
        copy.wait()


def scale_terms(rep, reps, cots, w2, dense, degree, terms):
    size = degree.shape[0]
    half = w2.shape[0] // reps
    at = pl.ds(pl.multiple_of(rep * half, half), half)
    pulled = dot(cots[...].reshape(size, -1), w2[at, :], (1, 1))
    scaled = (pulled / degree).astype(BF16)
    scaled_t = scaled.astype(F32).T.astype(BF16)
    for s in range(SPAN):
        part = dot(scaled_t, dense[:, s * size:(s + 1) * size], (1, 0))
        if s == HOPS:
            own = part.T + scaled.astype(F32)
        terms[s] = part.astype(BF16)
    return own


def front_kernel(rows, reps, blocks, tile, tiles, cols, row_ids, band_ids, band,
                 dense, first_o, deg_o):
    row = lax.axis_index("row")
    total = rows * blocks
    per = tiles.shape[2]
    dense[...] = jnp.zeros_like(dense)
    for b in range(blocks):
        at = pl.ds(b * tile, tile)
        ids = row_ids[at, :]
        sums = jnp.ones((tile, 1), F32)
        for j in range(reps):
            for k in range(per):
                slot = lax.rem(cols[j, b, k] + total - (row - HOPS) * blocks, total)
                same = ids == band_ids[pl.ds(slot, 1), :]
                value = jnp.where(same, tiles[j, b, k].astype(F32), 0.0)
                sums = sums + jnp.sum(value, axis=1, keepdims=True)
                dense[at, pl.ds(pl.multiple_of(slot * tile, tile), tile)] = value.astype(BF16)
        deg_o[at, :] = sums
    degree = deg_o[...]
    local = blocks * tile
    flat = band[...].reshape(SPAN * local, -1)
    summed = dot(dense[...], flat, (1, 0))
    first = ((summed + band[HOPS].astype(F32)) / degree).astype(BF16)
    first_o[...] = first


def full_front_kernel(rows, reps, blocks, tile, tiles, cols, row_ids, band_ids, band, cots, w2,
                      dense, first_o, terms_o, own_o, deg_o):
    front_kernel(rows, reps, blocks, tile, tiles, cols, row_ids, band_ids, band, dense, first_o, deg_o)
    own_o[...] = scale_terms(lax.axis_index("rep"), reps, cots, w2, dense, deg_o[...], terms_o)


def band_kernel(rows, first, terms, first_band, term_band, pair, joint, send, recv, local):
    flip, far, at = places(rows)
    greet([at(2), at(-2), at(far), at(flip)])
    joined = [remote(terms.at[HOPS + shift + flip], pair.at[n], send, recv, n, at(flip))
              for n, shift in enumerate((2, -2))]
    for copy in joined:
        copy.start()
    direct = [remote(terms.at[HOPS + far], term_band.at[2], send, recv, 2, at(far))]
    direct[0].start()
    moved = start_rows(rows, first, first_band, send, recv, 3)
    keep = pltpu.make_async_copy(first, first_band.at[HOPS], local.at[0])
    keep.start()
    direct.append(remote(terms.at[HOPS + flip], term_band.at[3], send, recv, 7, at(flip)))
    direct[1].start()
    for n, shift in enumerate((2, -2)):
        joined[n].wait_recv()
        joint[n] = (terms[HOPS + shift].astype(F32) + pair[n].astype(F32)).astype(BF16)
        step = remote(joint.at[n], term_band.at[n], send, recv, 8 + n, at(shift))
        step.start()
        direct.append(step)
    finish_rows(rows, moved, first_band, send, recv, 10)
    keep.wait()
    for copy in joined:
        copy.wait_send()
    for copy in direct:
        copy.wait()


def back_kernel(reps, dense, first_band, term_band, w1, own, deg, cots, second_o, grads_o):
    rep = lax.axis_index("rep")
    local, half = own.shape
    weight = w1[:, pl.ds(pl.multiple_of(rep * half, half), half)]
    preact = dot(first_band[HOPS], weight, (1, 0))
    mine = jnp.maximum(preact, 0.0).astype(BF16)
    summed = mine.astype(F32)
    for s in range(SPAN):
        hidden = mine if s == HOPS else jnp.maximum(dot(first_band[s], weight, (1, 0)), 0.0).astype(BF16)
        summed = summed + dot(dense[:, s * local:(s + 1) * local], hidden, (1, 0))
    second = (summed / deg[...]).astype(BF16)
    second_o[...] = second
    out = dot(second, cots[...].reshape(local, -1), (0, 0))
    width = out.shape[1] // half
    for i in range(width):
        grads_o[i * half:(i + 1) * half, :] = out[:, i * half:(i + 1) * half]
    got = term_band[0].astype(F32)
    for i in range(1, 4):
        got = got + term_band[i].astype(F32)
    back = got.T + own[...]
    delta = jnp.where(preact > 0.0, back, 0.0).astype(BF16)
    grads_o[width * half:, :] = dot(first_band[HOPS], delta, (0, 0))


def swap_kernel(reps, second, full, send, recv, local):
    row, rep = lax.axis_index("row"), lax.axis_index("rep")
    others = [(row, lax.rem(rep + t, reps)) for t in range(1, reps)]
    greet(others)
    copies = [remote(second.at[peer[1]], full.at[rep], send, recv, n, peer) for n, peer in enumerate(others)]
    copies.append(pltpu.make_async_copy(second.at[rep], full.at[rep], local.at[0]))
    for copy in copies:
        copy.start()
    for copy in copies:
        copy.wait()


def fused_kernel(feats, tiles, cols, sizes, w1, w2, cot, second_o, whole,
                 band, raw, masked, cots, w1_v, w2_v, cols_v, cols_s, firsts, hidden, terms, deg_v, pulled,
                 second_s, second_in, gi_out, gi_in, part, paired, total, parcel, parts,
                 send, recv, local):
    row, rep = lax.axis_index("row"), lax.axis_index("rep")
    rows, graphs = 16, sizes.shape[0]
    chip, core = row // 2, lax.rem(row, 2)
    other = 1 - rep
    flip, far, at = places(rows)
    mate, sibling = (row, other), at(flip)
    deep, mid, low = chip // 4, lax.rem(chip // 2, 2), lax.rem(chip, 2)
    peers, order = [], []
    for m in range(1, 8):
        q = lax.rem(deep + m // 4, 2) * 4 + lax.rem(mid + m // 2 % 2, 2) * 2 + lax.rem(low + m % 2, 2)
        order.append(q)
        peers.append((q * 2 + core, rep))
    used = [0]

    def push(src, dst, peer):
        n = used[0]
        used[0] = n + 1
        copy = remote(src, dst, send, recv, n, peer)
        copy.start()
        return copy

    taken = [0]

    def pull(src, dst):
        n = taken[0]
        taken[0] = n + 1
        copy = pltpu.make_async_copy(src, dst, local.at[n])
        copy.start()
        return copy

    got_cols = pull(cols, cols_s.at[rep])
    got_tiles = pull(tiles.at[pl.ds(rep * 2, 2)], raw.at[rep])
    got_cot = pull(cot, cots.at[rep])
    got_w2 = pull(w2, w2_v)
    got_w1 = [pull(w1.at[:, h * 256:(h + 1) * 256], w1_v.at[h]) for h in range(2)]
    got_feats = pull(feats, band.at[pl.ds(HOPS * 4, 4)])

    greet(peers + [at(far), sibling, mate])
    sent = []
    came_cols = push(cols, cols_v, mate)
    near = [push(feats, band.at[pl.ds((HOPS - shift) * 4, 4)], at(shift)) for shift in (2, -2)]
    direct = [push(feats, band.at[pl.ds((HOPS - shift) * 4, 4)], at(shift)) for shift in (far, flip)]
    came_tiles = [push(tiles.at[other * 2 + b], raw.at[rep, b], mate) for b in range(2)]
    sent += near + direct + came_tiles + [came_cols]

    ends, upto = [], jnp.int32(0)
    for g in range(graphs):
        upto = upto + sizes[g]
        ends.append(upto)

    def graph_of(spots):
        found = jnp.zeros(spots.shape, jnp.int32)
        for end in ends:
            found = found + (spots >= end).astype(jnp.int32)
        return found

    down = lax.broadcasted_iota(jnp.int32, (128, 128), 0)
    along = lax.broadcasted_iota(jnp.int32, (8, 128), 1)
    row_ids = [graph_of(down + (row * 4 + rep * 2 + b) * 128) for b in range(2)]

    def mask(j, b):
        for k in range(4):
            col = cols_s[j, rep * 2 + b, k]
            ids = graph_of(along + col * 128)[:1, :]
            value = jnp.where(row_ids[b] == ids, raw[j, b, k].astype(F32), 0.0).astype(BF16)
            masked[b, pl.ds(pl.multiple_of(j * 512 + k * 128, 128), 128), :] = value.T

    got_cols.wait()
    got_tiles.wait()
    for b in range(2):
        mask(rep, b)
    got_cot.wait()
    got_w2.wait()
    pulled[...] = dot(cots[rep], w2_v[...], (1, 1))

    came_cols.wait_recv()
    more_cols = pull(cols_v, cols_s.at[other])
    passed = []

    def hand_on(n, shift):
        near[n].wait_recv()
        spot = band.at[pl.ds((HOPS - shift) * 4, 4)]
        passed.append(push(spot, band.at[pl.ds((HOPS - shift - flip) * 4, 4)], sibling))

    more_cols.wait()
    for n, shift in enumerate((2, -2)):
        hand_on(n, shift)
    for b in range(2):
        came_tiles[b].wait_recv()
        mask(other, b)
    came_cot = push(cot, cots.at[rep], mate)
    sent.append(came_cot)
    ones = jnp.ones((1024, 128), BF16)
    for b in range(2):
        deg_v[b] = 1.0 + dot(masked[b], ones, (0, 0))
    got_feats.wait()
    for copy in direct + passed:
        copy.wait_recv()
    sent += passed

    def slot_of(b, n):
        return jnp.clip(lax.rem(cols_s[n // 4, rep * 2 + b, n % 4] + 64 - (row - HOPS) * 4, 64), 0, 27)

    for b in range(2):
        near_x = jnp.concatenate([band[slot_of(b, n)] for n in range(8)], axis=0)
        mine = band[HOPS * 4 + rep * 2 + b].astype(F32)
        first = ((dot(masked[b], near_x, (0, 0)) + mine) / deg_v[b]).astype(BF16)
        firsts[HOPS * 4 + rep * 2 + b] = first

    def span(s, p):
        return firsts.at[pl.ds(s * 4 + p * 2, 2)]

    own_half = span(HOPS, rep)
    across = push(own_half, own_half, mate)
    near = [push(own_half, span(HOPS - shift, rep), at(shift)) for shift in (2, -2)]
    direct = [push(own_half, span(HOPS - shift, rep), at(shift)) for shift in (far, flip)]
    sent += [across] + near + direct

    def tall(ref, s, p):
        return jnp.concatenate([ref[s * 4 + p * 2 + b] for b in range(2)], axis=0)

    def hide(s, p):
        x = tall(firsts, s, p)
        for h in range(2):
            value = jnp.maximum(dot(x, w1_v[h], (1, 0)), 0.0).astype(BF16)
            hidden[h, pl.ds(s * 4 + p * 2, 2)] = value.reshape(2, 128, 256)

    for copy in got_w1:
        copy.wait()
    hide(HOPS, rep)
    for b in range(2):
        scaled = (pulled[b * 128:(b + 1) * 128, :] / jnp.tile(deg_v[b], (1, 4))).astype(BF16)
        for h in range(2):
            piece = scaled[:, h * 256:(h + 1) * 256]
            part_h = dot(masked[b], piece, (1, 0))
            terms[h, b, :128, :] = (part_h[:128, :] + piece.astype(F32)).astype(BF16)
            terms[h, b, 128:, :] = part_h[128:, :].astype(BF16)

    across.wait_recv()
    handed = [push(span(HOPS, other), span(HOPS - flip, other), sibling)]
    hide(HOPS, other)
    direct[1].wait_recv()
    hide(HOPS + flip, rep)
    crossed = []
    for n, shift in enumerate((2, -2)):
        near[n].wait_recv()
        here = span(HOPS - shift, rep)
        crossed.append(push(here, here, mate))
        handed.append(push(here, span(HOPS - shift - flip, rep), sibling))
        hide(HOPS - shift, rep)
    direct[0].wait_recv()
    there = span(HOPS + far, rep)
    crossed.append(push(there, there, mate))
    hide(HOPS + far, rep)
    handed[0].wait_recv()
    hide(HOPS + flip, other)
    for n, shift in enumerate((2, -2)):
        handed[1 + n].wait_recv()
        hide(HOPS - shift + flip, rep)
    for n, shift in enumerate((2, -2)):
        crossed[n].wait_recv()
        here = span(HOPS - shift, other)
        handed.append(push(here, span(HOPS - shift - flip, other), sibling))
        hide(HOPS - shift, other)
    crossed[2].wait_recv()
    hide(HOPS + far, other)
    for n, shift in enumerate((2, -2)):
        handed[3 + n].wait_recv()
        hide(HOPS - shift + flip, other)
    sent += crossed + handed

    def forward(h):
        for b in range(2):
            near_h = jnp.concatenate([hidden[h, slot_of(b, n)] for n in range(8)], axis=0)
            mine = hidden[h, HOPS * 4 + rep * 2 + b].astype(F32)
            value = (dot(masked[b], near_h, (0, 0)) + mine) / jnp.tile(deg_v[b], (1, 2))
            second_s[h, b * 128:(b + 1) * 128, :] = value.astype(BF16)

    def weigh(h):
        for b in range(2):
            near_f = jnp.concatenate([firsts[slot_of(b, n)] for n in range(8)], axis=0)
            near_h = jnp.concatenate([hidden[h, slot_of(b, n)] for n in range(8)], axis=0)
            delta = jnp.where(near_h > 0, terms[h, b], jnp.zeros_like(near_h))
            value = dot(near_f, delta, (0, 0))
            grad = value if b == 0 else grad + value
        return grad

    forward(other)
    came_second = push(second_s.at[other], second_in, mate)
    gi_out[...] = weigh(other).astype(BF16)
    came_gi = push(gi_out, gi_in, mate)
    forward(rep)
    sent += [came_second, came_gi]
    gi = weigh(rep)
    for h in range(2):
        second_o[h] = second_s[h]
    came_cot.wait_recv()
    go = dot(second_s[rep], cots[rep], (0, 0))
    came_second.wait_recv()
    go = go + dot(second_in[...], cots[other], (0, 0))
    for s in range(16):
        j, q = s // 4, s % 4
        part[s // 8, s % 8, :64, :] = go[q * 64:(q + 1) * 64, j * 128:(j + 1) * 128]
    came_gi.wait_recv()
    gi = gi + gi_in[...].astype(F32)
    for s in range(16):
        j, q = s // 8, s % 8
        part[s // 8, s % 8, 64:, :] = gi[q * 16:(q + 1) * 16, j * 128:(j + 1) * 128]
    joined = push(part.at[1 - core], paired, sibling)
    joined.wait_recv()
    sent.append(joined)
    total[...] = part[core] + paired[...]
    parcel[...] = total[...].astype(BF16)
    shares = [push(parcel.at[q], parts.at[t], peer) for t, (q, peer) in enumerate(zip(order, peers))]
    value = total[chip]
    for t, copy in enumerate(shares):
        copy.wait_recv()
        value = value + parts[t].astype(F32)
    sent += shares
    whole[rep, core, chip] = value.astype(BF16)

    def spot(p, c, q):
        return whole.at[p, c, q]

    def spread(p, c, q, peer):
        return push(spot(p, c, q), spot(p, c, q), peer)

    beyond = [spread(rep, core, chip, mate)]
    rounds = [spread(rep, core, chip, peer) for peer in peers]
    aside = [spread(rep, core, chip, sibling)]
    for t, copy in enumerate(rounds):
        copy.wait_recv()
        beyond.append(spread(rep, core, order[t], mate))
        aside.append(spread(rep, core, order[t], sibling))
    for t, copy in enumerate(beyond):
        copy.wait_recv()
        aside.append(spread(other, core, chip if t == 0 else order[t - 1], sibling))
    for copy in aside:
        copy.wait_recv()
    for copy in sent + beyond + rounds + aside:
        copy.wait_send()


def end_kernel(second, whole, w2, scores_o, gi_o, go_o):
    total = dot(second[0], w2[:256, :], (1, 0)) + dot(second[1], w2[256:, :], (1, 0))
    scores_o[...] = total.astype(BF16)
    for p in range(2):
        for s in range(16):
            piece = whole[p, s // 8, s % 8].astype(F32)
            j, q = s // 4, s % 4
            go_o[p * 256 + q * 64:p * 256 + (q + 1) * 64, j * 128:(j + 1) * 128] = piece[:64]
            j, q = s // 8, s % 8
            gi_o[q * 16:(q + 1) * 16, p * 256 + j * 128:p * 256 + (j + 1) * 128] = piece[64:]


def fused(features, input_weight, output_weight, cotangent, adjacency_tiles, block_columns, graph_sizes):
    second, whole = pl.pallas_call(
        fused_kernel,
        out_shape=(shape((2, 256, 256), BF16), shape((2, 2, 8, 80, 128), BF16)),
        in_specs=[HBM, HBM, HBM, SMEM, HBM, HBM, HBM],
        out_specs=(VMEM,) * 2,
        scratch_shapes=[
            pltpu.VMEM((28, 128, 128), BF16),
            pltpu.VMEM((2, 2, 4, 128, 128), BF16),
            pltpu.VMEM((2, 1024, 128), BF16),
            pltpu.VMEM((2, 256, 512), BF16),
            pltpu.VMEM((2, 128, 256), BF16),
            pltpu.VMEM((512, 512), BF16),
            pltpu.VMEM((4, 4), jnp.int32),
            pltpu.SMEM((2, 4, 4), jnp.int32),
            pltpu.VMEM((28, 128, 128), BF16),
            pltpu.VMEM((2, 28, 128, 256), BF16),
            pltpu.VMEM((2, 2, 1024, 256), BF16),
            pltpu.VMEM((2, 128, 128), F32),
            pltpu.VMEM((256, 512), F32),
            pltpu.VMEM((2, 256, 256), BF16),
            pltpu.VMEM((256, 256), BF16),
            pltpu.VMEM((128, 256), BF16),
            pltpu.VMEM((128, 256), BF16),
            pltpu.VMEM((2, 8, 80, 128), F32),
            pltpu.VMEM((8, 80, 128), F32),
            pltpu.VMEM((8, 80, 128), F32),
            pltpu.VMEM((8, 80, 128), BF16),
            pltpu.VMEM((7, 80, 128), BF16),
            pltpu.SemaphoreType.DMA((72,)),
            pltpu.SemaphoreType.DMA((72,)),
            pltpu.SemaphoreType.DMA((8,)),
        ],
        compiler_params=params(0),
    )(features.reshape(4, 128, 128), adjacency_tiles, block_columns, graph_sizes, input_weight, output_weight,
      cotangent)
    return pl.pallas_call(
        end_kernel,
        out_shape=(shape((256, 512), BF16), shape((128, 512), F32), shape((512, 512), F32)),
        in_specs=[VMEM] * 3,
        out_specs=(VMEM,) * 3,
        compiler_params=params(),
    )(second, whole, output_weight)


def params(number=None):
    limit = 48 << 20
    if number is None:
        return pltpu.CompilerParams(vmem_limit_bytes=limit)
    return pltpu.CompilerParams(vmem_limit_bytes=limit, collective_id=number, has_side_effects=True)


def shape(dims, kind):
    return jax.ShapeDtypeStruct(dims, kind)


def sems(count):
    return [pltpu.SemaphoreType.DMA((count,)), pltpu.SemaphoreType.DMA((count,)), pltpu.SemaphoreType.DMA((4,))]


def body(
    features, input_weight, output_weight, cotangent, adjacency_tiles, block_columns, graph_sizes
):
    row = lax.axis_index("row")
    rows, reps = lax.axis_size("row"), lax.axis_size("rep")
    blocks, per, tile = adjacency_tiles.shape[:3]
    local = blocks * tile
    fin = features.shape[1]
    hid = output_weight.shape[0]
    half, quarter = hid // reps, local // reps
    nodes = rows * local
    if (rows, reps, blocks, per) == (16, 2, 4, 4) and graph_sizes.shape[0] <= 32:
        return fused(features, input_weight, output_weight, cotangent, adjacency_tiles, block_columns, graph_sizes)
    upto = jnp.arange(graph_sizes.shape[0])
    ends = jnp.sum(jnp.where(upto[None, :] <= upto[:, None], graph_sizes[None, :], 0), axis=1)

    def graph_of(places):
        return jnp.sum((places[..., None] >= ends).astype(jnp.int32), axis=-1)

    spots = lax.rem((row - HOPS) * local + nodes + jnp.arange(SPAN * local, dtype=jnp.int32), nodes)
    ids = graph_of(spots)
    row_ids = ids[HOPS * local:(HOPS + 1) * local].reshape(local, 1)
    band_ids = ids.reshape(SPAN * blocks, tile)
    padded = jnp.pad(block_columns, ((0, 8 - blocks), (0, 128 - per)))
    tall = hid * hid // reps // half + fin
    band, cots, all_tiles, all_cols = pl.pallas_call(
        functools.partial(open_kernel, rows, reps),
        out_shape=(
            shape((SPAN, local, fin), BF16),
            shape((reps, quarter, hid), BF16),
            shape((reps,) + adjacency_tiles.shape, BF16),
            shape((reps, 8, 128), jnp.int32),
        ),
        in_specs=[HBM] * 4,
        out_specs=(VMEM,) * 3 + (ANY,),
        scratch_shapes=sems(3 * (reps - 1) + 6),
        compiler_params=params(0),
    )(features, cotangent, adjacency_tiles, padded)
    dense, first, terms, own, degree = pl.pallas_call(
        functools.partial(full_front_kernel, rows, reps, blocks, tile),
        out_shape=(
            shape((local, SPAN * local), BF16),
            shape((local, fin), BF16),
            shape((SPAN, half, local), BF16),
            shape((local, half), F32),
            shape((local, 1), F32),
        ),
        in_specs=[VMEM, SMEM] + [VMEM] * 5,
        out_specs=(VMEM,) * 5,
        compiler_params=params(),
    )(all_tiles, all_cols, row_ids, band_ids, band, cots, output_weight)
    first_band, term_band = pl.pallas_call(
        functools.partial(band_kernel, rows),
        out_shape=(shape((SPAN, local, fin), BF16), shape((4, half, local), BF16)),
        in_specs=[VMEM] * 2,
        out_specs=(VMEM,) * 2,
        scratch_shapes=[pltpu.VMEM((2, half, local), BF16)] * 2 + sems(12),
        compiler_params=params(1),
    )(first, terms)
    second, grads = pl.pallas_call(
        functools.partial(back_kernel, reps),
        out_shape=(shape((local, half), BF16), shape((tall, half), F32)),
        in_specs=[VMEM] * 7,
        out_specs=(VMEM,) * 2,
        compiler_params=params(),
    )(dense, first_band, term_band, input_weight, own, degree, cots)
    second = second.reshape(reps, quarter, half)
    full = pl.pallas_call(
        functools.partial(swap_kernel, reps),
        out_shape=shape((reps, quarter, half), BF16),
        in_specs=[ANY],
        out_specs=ANY,
        scratch_shapes=sems(reps),
        compiler_params=params(2),
    )(second)
    whole = lax.all_gather(lax.psum(grads, "row"), "rep", axis=0)
    scores = dot(full.transpose(1, 0, 2).reshape(quarter, hid), output_weight, (1, 0)).astype(BF16)
    grad_input = whole[:, tall - fin:].transpose(1, 0, 2).reshape(fin, hid)
    grad_output = whole[:, :tall - fin].reshape(reps, hid // half, half, half)
    grad_output = grad_output.transpose(0, 2, 1, 3).reshape(hid, hid)
    return scores, grad_input, grad_output


def solution(mesh):
    placed = (
        P("row", None),
        P(),
        P(),
        P(("row", "rep"), None),
        P("row", "rep", None, None),
        P("row", "rep"),
        P(),
    )
    return jax.shard_map(
        body,
        mesh=mesh,
        in_specs=placed,
        out_specs=(P(("row", "rep"), None), P(), P()),
        check_vma=False,
    )
```

```python
import functools

import jax
import jax.numpy as jnp
from jax import lax
from jax.experimental import pallas as pl
from jax.experimental.pallas import tpu as pltpu
from jax.sharding import PartitionSpec as P

HOPS = 3
SPAN = 2 * HOPS + 1
MESH = pl.DeviceIdType.MESH
ANY = pl.BlockSpec(memory_space=pl.ANY)
HBM = pl.BlockSpec(memory_space=pltpu.HBM)
VMEM = pl.BlockSpec(memory_space=pltpu.VMEM)
SMEM = pl.BlockSpec(memory_space=pltpu.SMEM)
F32 = jnp.float32
BF16 = jnp.bfloat16


def dot(a, b, dims):
    return lax.dot_general(a, b, ((dims[:1], dims[1:]), ((), ())), preferred_element_type=F32)


def greet(peers):
    barrier = pltpu.get_barrier_semaphore()
    for peer in peers:
        pl.semaphore_signal(barrier, inc=1, device_id=peer, device_id_type=MESH)
    pl.semaphore_wait(barrier, len(peers))


def remote(src, dst, send, recv, index, peer):
    return pltpu.make_async_remote_copy(
        src_ref=src, dst_ref=dst, send_sem=send.at[index], recv_sem=recv.at[index],
        device_id=peer, device_id_type=MESH,
    )


def places(rows):
    row, rep = lax.axis_index("row"), lax.axis_index("rep")
    core = lax.rem(row, 2)
    flip, far = 1 - 2 * core, 6 * core - 3

    def at(shift):
        return (lax.rem(row + shift + rows, rows), rep)

    return flip, far, at


def start_rows(rows, src, band, send, recv, base):
    flip, far, at = places(rows)
    copies = [remote(src, band.at[HOPS - shift], send, recv, base + n, at(shift))
              for n, shift in enumerate((2, -2, far, flip))]
    for copy in copies:
        copy.start()
    return copies


def finish_rows(rows, copies, band, send, recv, base):
    flip, far, at = places(rows)
    passed = []
    for n, shift in enumerate((2, -2)):
        copies[n].wait_recv()
        step = remote(band.at[HOPS - shift], band.at[HOPS - shift - flip], send, recv, base + n, at(flip))
        step.start()
        passed.append(step)
    for copy in copies[2:]:
        copy.wait_recv()
    for copy in copies:
        copy.wait_send()
    for copy in passed:
        copy.wait()


def open_kernel(rows, reps, feats, cot, tiles, cols, band, cots, all_tiles, all_cols, send, recv, local):
    row, rep = lax.axis_index("row"), lax.axis_index("rep")
    flip, far, at = places(rows)
    others = [(row, lax.rem(rep + t, reps)) for t in range(1, reps)]
    greet([at(2), at(-2), at(far), at(flip)] + others)
    copies, n = [], 0
    pieces = ((tiles, all_tiles), (cols, all_cols), (cot, cots))
    pieces = pieces if cot is not None else pieces[:2]
    for peer in others:
        for src, dst in pieces:
            copies.append(remote(src, dst.at[rep], send, recv, n, peer))
            n += 1
    for i, (src, dst) in enumerate(pieces):
        copies.append(pltpu.make_async_copy(src, dst.at[rep], local.at[i]))
    copies.append(pltpu.make_async_copy(feats, band.at[HOPS], local.at[3]))
    for copy in copies:
        copy.start()
    moved = start_rows(rows, feats, band, send, recv, n)
    finish_rows(rows, moved, band, send, recv, n + 4)
    for copy in copies:
        copy.wait()


def scale_terms(rep, reps, cots, w2, dense, degree, terms):
    size = degree.shape[0]
    half = w2.shape[0] // reps
    at = pl.ds(pl.multiple_of(rep * half, half), half)
    pulled = dot(cots[...].reshape(size, -1), w2[at, :], (1, 1))
    scaled = (pulled / degree).astype(BF16)
    scaled_t = scaled.astype(F32).T.astype(BF16)
    for s in range(SPAN):
        part = dot(scaled_t, dense[:, s * size:(s + 1) * size], (1, 0))
        if s == HOPS:
            own = part.T + scaled.astype(F32)
        terms[s] = part.astype(BF16)
    return own


def front_kernel(rows, reps, blocks, tile, tiles, cols, row_ids, band_ids, band,
                 dense, first_o, deg_o):
    row = lax.axis_index("row")
    total = rows * blocks
    per = tiles.shape[2]
    dense[...] = jnp.zeros_like(dense)
    for b in range(blocks):
        at = pl.ds(b * tile, tile)
        ids = row_ids[at, :]
        sums = jnp.ones((tile, 1), F32)
        for j in range(reps):
            for k in range(per):
                slot = lax.rem(cols[j, b, k] + total - (row - HOPS) * blocks, total)
                same = ids == band_ids[pl.ds(slot, 1), :]
                value = jnp.where(same, tiles[j, b, k].astype(F32), 0.0)
                sums = sums + jnp.sum(value, axis=1, keepdims=True)
                dense[at, pl.ds(pl.multiple_of(slot * tile, tile), tile)] = value.astype(BF16)
        deg_o[at, :] = sums
    degree = deg_o[...]
    local = blocks * tile
    flat = band[...].reshape(SPAN * local, -1)
    summed = dot(dense[...], flat, (1, 0))
    first = ((summed + band[HOPS].astype(F32)) / degree).astype(BF16)
    first_o[...] = first


def full_front_kernel(rows, reps, blocks, tile, tiles, cols, row_ids, band_ids, band, cots, w2,
                      dense, first_o, terms_o, own_o, deg_o):
    front_kernel(rows, reps, blocks, tile, tiles, cols, row_ids, band_ids, band, dense, first_o, deg_o)
    own_o[...] = scale_terms(lax.axis_index("rep"), reps, cots, w2, dense, deg_o[...], terms_o)


def band_kernel(rows, first, terms, first_band, term_band, pair, joint, send, recv, local):
    flip, far, at = places(rows)
    greet([at(2), at(-2), at(far), at(flip)])
    joined = [remote(terms.at[HOPS + shift + flip], pair.at[n], send, recv, n, at(flip))
              for n, shift in enumerate((2, -2))]
    for copy in joined:
        copy.start()
    direct = [remote(terms.at[HOPS + far], term_band.at[2], send, recv, 2, at(far))]
    direct[0].start()
    moved = start_rows(rows, first, first_band, send, recv, 3)
    keep = pltpu.make_async_copy(first, first_band.at[HOPS], local.at[0])
    keep.start()
    direct.append(remote(terms.at[HOPS + flip], term_band.at[3], send, recv, 7, at(flip)))
    direct[1].start()
    for n, shift in enumerate((2, -2)):
        joined[n].wait_recv()
        joint[n] = (terms[HOPS + shift].astype(F32) + pair[n].astype(F32)).astype(BF16)
        step = remote(joint.at[n], term_band.at[n], send, recv, 8 + n, at(shift))
        step.start()
        direct.append(step)
    finish_rows(rows, moved, first_band, send, recv, 10)
    keep.wait()
    for copy in joined:
        copy.wait_send()
    for copy in direct:
        copy.wait()


def back_kernel(reps, dense, first_band, term_band, w1, own, deg, cots, second_o, grads_o):
    rep = lax.axis_index("rep")
    local, half = own.shape
    weight = w1[:, pl.ds(pl.multiple_of(rep * half, half), half)]
    preact = dot(first_band[HOPS], weight, (1, 0))
    mine = jnp.maximum(preact, 0.0).astype(BF16)
    summed = mine.astype(F32)
    for s in range(SPAN):
        hidden = mine if s == HOPS else jnp.maximum(dot(first_band[s], weight, (1, 0)), 0.0).astype(BF16)
        summed = summed + dot(dense[:, s * local:(s + 1) * local], hidden, (1, 0))
    second = (summed / deg[...]).astype(BF16)
    second_o[...] = second
    out = dot(second, cots[...].reshape(local, -1), (0, 0))
    width = out.shape[1] // half
    for i in range(width):
        grads_o[i * half:(i + 1) * half, :] = out[:, i * half:(i + 1) * half]
    got = term_band[0].astype(F32)
    for i in range(1, 4):
        got = got + term_band[i].astype(F32)
    back = got.T + own[...]
    delta = jnp.where(preact > 0.0, back, 0.0).astype(BF16)
    grads_o[width * half:, :] = dot(first_band[HOPS], delta, (0, 0))


def swap_kernel(reps, second, full, send, recv, local):
    row, rep = lax.axis_index("row"), lax.axis_index("rep")
    others = [(row, lax.rem(rep + t, reps)) for t in range(1, reps)]
    greet(others)
    copies = [remote(second.at[peer[1]], full.at[rep], send, recv, n, peer) for n, peer in enumerate(others)]
    copies.append(pltpu.make_async_copy(second.at[rep], full.at[rep], local.at[0]))
    for copy in copies:
        copy.start()
    for copy in copies:
        copy.wait()


class Flight:
    def __init__(self, copy):
        self.copy, self.landed = copy, False
        copy.start()

    def wait_recv(self):
        if not self.landed:
            self.copy.wait_recv()
        self.landed = True

    def wait(self):
        if not self.landed:
            self.copy.wait()
        self.landed = True


def fused_kernel(feats, tiles, cols, sizes, w1, w2, cot, scores_o, whole,
                 band, raw, masked, cots, w1_v, w2_v, cols_v, cols_s, firsts, hidden, terms, deg_v,
                 second_s, second_in, part, paired, total, parcel, parts, send, recv, local):
    row, rep = lax.axis_index("row"), lax.axis_index("rep")
    graphs = sizes.shape[0]
    chip, core = row // 2, lax.rem(row, 2)
    other = 1 - rep
    flip, far, at = places(16)
    mate, sibling = (row, other), at(flip)
    deep, mid, low = chip // 4, lax.rem(chip // 2, 2), lax.rem(chip, 2)
    peers, order = [], []
    for m in range(1, 8):
        q = lax.rem(deep + m // 4, 2) * 4 + lax.rem(mid + m // 2 % 2, 2) * 2 + lax.rem(low + m % 2, 2)
        order.append(q)
        peers.append((q * 2 + core, rep))
    flights, pulls = [], []

    def push(src, dst, peer):
        flights.append(Flight(remote(src, dst, send, recv, len(flights), peer)))
        return flights[-1]

    def pull(src, dst):
        pulls.append(Flight(pltpu.make_async_copy(src, dst, local.at[len(pulls)])))
        return pulls[-1]

    half = pl.ds(pl.multiple_of(rep * 256, 256), 256)
    got_cols = pull(cols, cols_s.at[rep])
    got_tiles = pull(tiles, raw.at[rep])
    got_cot = pull(cot, cots.at[rep])
    got_w2 = pull(w2, w2_v)
    got_w1 = pull(w1.at[:, half], w1_v)
    got_feats = pull(feats, band.at[pl.ds(HOPS * 4, 4)])

    def send_tile(b):
        return push(tiles.at[b], raw.at[rep, b], mate)

    def group(ref, s):
        return ref.at[pl.ds(s * 4, 4)]

    greet(peers + [at(far), sibling, mate])
    came_cols = push(cols, cols_v, mate)
    near = [push(feats, group(band, HOPS - shift), at(shift)) for shift in (2, -2)]
    direct = [push(feats, group(band, HOPS - shift), at(shift)) for shift in (far, flip)]
    came_mine = [send_tile(other * 2 + b) for b in range(2)]

    ends, upto = [], jnp.int32(0)
    for g in range(graphs):
        upto = upto + sizes[g]
        ends.append(upto)

    def graph_of(spots):
        found = jnp.zeros(spots.shape, jnp.int32)
        for end in ends:
            found = found + (spots >= end).astype(jnp.int32)
        return found

    down = lax.broadcasted_iota(jnp.int32, (128, 128), 0)
    along = lax.broadcasted_iota(jnp.int32, (8, 128), 1)
    mine = [rep * 2, rep * 2 + 1]
    theirs = [other * 2, other * 2 + 1]

    def mask(j, b):
        row_ids = graph_of(down + (row * 4 + b) * 128)
        for k in range(4):
            ids = graph_of(along + cols_s[j, b, k] * 128)[:1, :]
            value = jnp.where(row_ids == ids, raw[j, b, k].astype(F32), 0.0).astype(BF16)
            masked[b, pl.ds(pl.multiple_of(j * 512 + k * 128, 128), 128), :] = value.T

    ones = jnp.ones((1024, 128), BF16)

    def count(b):
        deg_v[b] = 1.0 + dot(masked[b], ones, (0, 0))

    def scale(p):
        pulled = dot(cots[p], w2_v[half, :], (1, 1))
        for i in range(2):
            b = p * 2 + i
            scaled = (pulled[i * 128:(i + 1) * 128, :] / jnp.tile(deg_v[b], (1, 2))).astype(BF16)
            value = dot(masked[b], scaled, (1, 0))
            terms[b, :128, :] = (value[:128, :] + scaled.astype(F32)).astype(BF16)
            terms[b, 128:, :] = value[128:, :].astype(BF16)

    def slot_of(b, n):
        return jnp.clip(lax.rem(cols_s[n // 4, b, n % 4] + 64 - (row - HOPS) * 4, 64), 0, 27)

    got_cols.wait()
    got_tiles.wait()
    for b in mine + theirs:
        mask(rep, b)
    came_cols.wait_recv()
    more_cols = pull(cols_v, cols_s.at[other])
    more_cols.wait()
    passed = []
    for n, shift in enumerate((2, -2)):
        near[n].wait_recv()
        passed.append(push(group(band, HOPS - shift), group(band, HOPS - shift - flip), sibling))
    for b in range(2):
        came_mine[b].wait_recv()
        mask(other, mine[b])
        count(mine[b])
    came_theirs = [send_tile(mine[0])]
    got_feats.wait()
    for copy in direct + passed:
        copy.wait_recv()
    for b in mine:
        near_x = jnp.concatenate([band[slot_of(b, n)] for n in range(8)], axis=0)
        value = dot(masked[b], near_x, (0, 0)) + band[HOPS * 4 + b].astype(F32)
        firsts[HOPS * 4 + b] = (value / deg_v[b]).astype(BF16)

    def span(s, p):
        return firsts.at[pl.ds(s * 4 + p * 2, 2)]

    def offer(p):
        return [push(span(HOPS, p), span(HOPS - shift, p), at(shift)) for shift in (2, -2, far, flip)]

    def hide(s):
        x = firsts[s * 4:(s + 1) * 4] if isinstance(s, int) else firsts[pl.ds(s * 4, 4)]
        value = jnp.maximum(dot(x.reshape(512, 128), w1_v[...], (1, 0)), 0.0).astype(BF16)
        hidden[pl.ds(s * 4, 4)] = value.reshape(4, 128, 256)

    across = push(span(HOPS, rep), span(HOPS, rep), mate)
    waves = [offer(rep)]
    got_cot.wait()
    got_w2.wait()
    got_w1.wait()
    across.wait_recv()
    waves.append(offer(other))
    came_theirs.append(send_tile(mine[1]))
    came_cot = push(cot, cots.at[rep], mate)
    scale(rep)
    hide(HOPS)
    handed = []
    for p, wave in zip((rep, other), waves):
        for n, shift in enumerate((2, -2)):
            wave[n].wait_recv()
            handed.append(push(span(HOPS - shift, p), span(HOPS - shift - flip, p), sibling))
    for wave in waves:
        wave[2].wait_recv()
        wave[3].wait_recv()
    for s in (HOPS + flip, HOPS - 2, HOPS + 2, HOPS + far):
        hide(s)
    for b in range(2):
        came_theirs[b].wait_recv()
        mask(other, theirs[b])
        count(theirs[b])
    came_cot.wait_recv()
    scale(other)
    for copy in handed:
        copy.wait_recv()
    for shift in (2, -2):
        hide(HOPS - shift + flip)

    for b in range(4):
        near_h = jnp.concatenate([hidden[slot_of(b, n)] for n in range(8)], axis=0)
        value = (dot(masked[b], near_h, (0, 0)) + hidden[HOPS * 4 + b].astype(F32)) / jnp.tile(deg_v[b], (1, 2))
        second_s[b // 2, (b % 2) * 128:(b % 2 + 1) * 128, :] = value.astype(BF16)
        near_f = jnp.concatenate([firsts[slot_of(b, n)] for n in range(8)], axis=0)
        value = dot(near_f, jnp.where(near_h > 0, terms[b], jnp.zeros_like(near_h)), (0, 0))
        gi = value if b == 0 else gi + value
    came_second = push(second_s.at[other], second_in, mate)
    go = dot(second_s[...].reshape(512, 256), cots[...].reshape(512, 512), (0, 0))
    for s in range(16):
        j, q = s // 4, s % 4
        part[s // 8, s % 8, :64, :] = go[q * 64:(q + 1) * 64, j * 128:(j + 1) * 128]
        j, q = s // 8, s % 8
        part[s // 8, s % 8, 64:, :] = gi[q * 16:(q + 1) * 16, j * 128:(j + 1) * 128]
    joined = push(part.at[1 - core], paired, sibling)
    joined.wait_recv()
    total[...] = part[core] + paired[...]
    parcel[...] = total[...].astype(BF16)
    shares = [push(parcel.at[q], parts.at[t], peer) for t, (q, peer) in enumerate(zip(order, peers))]
    came_second.wait_recv()
    scores = dot(second_s[rep], w2_v[half, :], (1, 0))
    scores = scores + dot(second_in[...], w2_v[pl.ds(pl.multiple_of(other * 256, 256), 256), :], (1, 0))
    scores_o[...] = scores.astype(BF16)
    value = total[chip]
    for t, copy in enumerate(shares):
        copy.wait_recv()
        value = value + parts[t].astype(F32)
    whole[rep, core, chip] = value.astype(BF16)

    def spread(p, c, q, peer):
        return push(whole.at[p, c, q], whole.at[p, c, q], peer)

    beyond = [spread(rep, core, chip, mate)]
    rounds = [spread(rep, core, chip, peer) for peer in peers]
    aside = [spread(rep, core, chip, sibling)]
    for t, copy in enumerate(rounds):
        copy.wait_recv()
        beyond.append(spread(rep, core, order[t], mate))
        aside.append(spread(rep, core, order[t], sibling))
    for t, copy in enumerate(beyond):
        copy.wait_recv()
        aside.append(spread(other, core, chip if t == 0 else order[t - 1], sibling))
    for copy in aside:
        copy.wait_recv()
    for flight in flights:
        flight.copy.wait_send()


def end_kernel(scores, whole, scores_o, gi_o, go_o):
    scores_o[...] = scores[...]
    for p in range(2):
        for s in range(16):
            piece = whole[p, s // 8, s % 8].astype(F32)
            j, q = s // 4, s % 4
            go_o[p * 256 + q * 64:p * 256 + (q + 1) * 64, j * 128:(j + 1) * 128] = piece[:64]
            j, q = s // 8, s % 8
            gi_o[q * 16:(q + 1) * 16, p * 256 + j * 128:p * 256 + (j + 1) * 128] = piece[64:]


def fused(features, input_weight, output_weight, cotangent, adjacency_tiles, block_columns, graph_sizes):
    scores, whole = pl.pallas_call(
        fused_kernel,
        out_shape=(pltpu.VMEM((256, 512), BF16), pltpu.VMEM((2, 2, 8, 80, 128), BF16)),
        in_specs=[HBM, HBM, HBM, SMEM, HBM, HBM, HBM],
        out_specs=(VMEM,) * 2,
        scratch_shapes=[
            pltpu.VMEM((28, 128, 128), BF16),
            pltpu.VMEM((2, 4, 4, 128, 128), BF16),
            pltpu.VMEM((4, 1024, 128), BF16),
            pltpu.VMEM((2, 256, 512), BF16),
            pltpu.VMEM((128, 256), BF16),
            pltpu.VMEM((512, 512), BF16),
            pltpu.VMEM((4, 4), jnp.int32),
            pltpu.SMEM((2, 4, 4), jnp.int32),
            pltpu.VMEM((28, 128, 128), BF16),
            pltpu.VMEM((28, 128, 256), BF16),
            pltpu.VMEM((4, 1024, 256), BF16),
            pltpu.VMEM((4, 128, 128), F32),
            pltpu.VMEM((2, 256, 256), BF16),
            pltpu.VMEM((256, 256), BF16),
            pltpu.VMEM((2, 8, 80, 128), F32),
            pltpu.VMEM((8, 80, 128), F32),
            pltpu.VMEM((8, 80, 128), F32),
            pltpu.VMEM((8, 80, 128), BF16),
            pltpu.VMEM((7, 80, 128), BF16),
            pltpu.SemaphoreType.DMA((72,)),
            pltpu.SemaphoreType.DMA((72,)),
            pltpu.SemaphoreType.DMA((8,)),
        ],
        compiler_params=pltpu.CompilerParams(vmem_limit_bytes=58 << 20, collective_id=0, has_side_effects=True),
    )(features.reshape(4, 128, 128), adjacency_tiles, block_columns, graph_sizes, input_weight, output_weight,
      cotangent)
    return pl.pallas_call(
        end_kernel,
        out_shape=(shape((256, 512), BF16), shape((128, 512), F32), shape((512, 512), F32)),
        in_specs=[VMEM] * 2,
        out_specs=(VMEM,) * 3,
        compiler_params=params(),
    )(scores, whole)


def params(number=None):
    limit = 48 << 20
    if number is None:
        return pltpu.CompilerParams(vmem_limit_bytes=limit)
    return pltpu.CompilerParams(vmem_limit_bytes=limit, collective_id=number, has_side_effects=True)


def shape(dims, kind):
    return jax.ShapeDtypeStruct(dims, kind)


def sems(count):
    return [pltpu.SemaphoreType.DMA((count,)), pltpu.SemaphoreType.DMA((count,)), pltpu.SemaphoreType.DMA((4,))]


def body(
    features, input_weight, output_weight, cotangent, adjacency_tiles, block_columns, graph_sizes
):
    row = lax.axis_index("row")
    rows, reps = lax.axis_size("row"), lax.axis_size("rep")
    blocks, per, tile = adjacency_tiles.shape[:3]
    local = blocks * tile
    fin = features.shape[1]
    hid = output_weight.shape[0]
    half, quarter = hid // reps, local // reps
    nodes = rows * local
    if (rows, reps, blocks, per) == (16, 2, 4, 4) and graph_sizes.shape[0] <= 32:
        return fused(features, input_weight, output_weight, cotangent, adjacency_tiles, block_columns, graph_sizes)
    upto = jnp.arange(graph_sizes.shape[0])
    ends = jnp.sum(jnp.where(upto[None, :] <= upto[:, None], graph_sizes[None, :], 0), axis=1)

    def graph_of(places):
        return jnp.sum((places[..., None] >= ends).astype(jnp.int32), axis=-1)

    spots = lax.rem((row - HOPS) * local + nodes + jnp.arange(SPAN * local, dtype=jnp.int32), nodes)
    ids = graph_of(spots)
    row_ids = ids[HOPS * local:(HOPS + 1) * local].reshape(local, 1)
    band_ids = ids.reshape(SPAN * blocks, tile)
    padded = jnp.pad(block_columns, ((0, 8 - blocks), (0, 128 - per)))
    tall = hid * hid // reps // half + fin
    band, cots, all_tiles, all_cols = pl.pallas_call(
        functools.partial(open_kernel, rows, reps),
        out_shape=(
            shape((SPAN, local, fin), BF16),
            shape((reps, quarter, hid), BF16),
            shape((reps,) + adjacency_tiles.shape, BF16),
            shape((reps, 8, 128), jnp.int32),
        ),
        in_specs=[HBM] * 4,
        out_specs=(VMEM,) * 3 + (ANY,),
        scratch_shapes=sems(3 * (reps - 1) + 6),
        compiler_params=params(0),
    )(features, cotangent, adjacency_tiles, padded)
    dense, first, terms, own, degree = pl.pallas_call(
        functools.partial(full_front_kernel, rows, reps, blocks, tile),
        out_shape=(
            shape((local, SPAN * local), BF16),
            shape((local, fin), BF16),
            shape((SPAN, half, local), BF16),
            shape((local, half), F32),
            shape((local, 1), F32),
        ),
        in_specs=[VMEM, SMEM] + [VMEM] * 5,
        out_specs=(VMEM,) * 5,
        compiler_params=params(),
    )(all_tiles, all_cols, row_ids, band_ids, band, cots, output_weight)
    first_band, term_band = pl.pallas_call(
        functools.partial(band_kernel, rows),
        out_shape=(shape((SPAN, local, fin), BF16), shape((4, half, local), BF16)),
        in_specs=[VMEM] * 2,
        out_specs=(VMEM,) * 2,
        scratch_shapes=[pltpu.VMEM((2, half, local), BF16)] * 2 + sems(12),
        compiler_params=params(1),
    )(first, terms)
    second, grads = pl.pallas_call(
        functools.partial(back_kernel, reps),
        out_shape=(shape((local, half), BF16), shape((tall, half), F32)),
        in_specs=[VMEM] * 7,
        out_specs=(VMEM,) * 2,
        compiler_params=params(),
    )(dense, first_band, term_band, input_weight, own, degree, cots)
    second = second.reshape(reps, quarter, half)
    full = pl.pallas_call(
        functools.partial(swap_kernel, reps),
        out_shape=shape((reps, quarter, half), BF16),
        in_specs=[ANY],
        out_specs=ANY,
        scratch_shapes=sems(reps),
        compiler_params=params(2),
    )(second)
    whole = lax.all_gather(lax.psum(grads, "row"), "rep", axis=0)
    scores = dot(full.transpose(1, 0, 2).reshape(quarter, hid), output_weight, (1, 0)).astype(BF16)
    grad_input = whole[:, tall - fin:].transpose(1, 0, 2).reshape(fin, hid)
    grad_output = whole[:, :tall - fin].reshape(reps, hid // half, half, half)
    grad_output = grad_output.transpose(0, 2, 1, 3).reshape(hid, hid)
    return scores, grad_input, grad_output


def solution(mesh):
    placed = (
        P("row", None),
        P(),
        P(),
        P(("row", "rep"), None),
        P("row", "rep", None, None),
        P("row", "rep"),
        P(),
    )
    return jax.shard_map(
        body,
        mesh=mesh,
        in_specs=placed,
        out_specs=(P(("row", "rep"), None), P(), P()),
        check_vma=False,
    )
```

```python
import functools

import jax
import jax.numpy as jnp
from jax import lax
from jax.experimental import pallas as pl
from jax.experimental.pallas import tpu as pltpu
from jax.sharding import PartitionSpec as P

HOPS = 3
SPAN = 2 * HOPS + 1
MESH = pl.DeviceIdType.MESH
ANY = pl.BlockSpec(memory_space=pl.ANY)
HBM = pl.BlockSpec(memory_space=pltpu.HBM)
VMEM = pl.BlockSpec(memory_space=pltpu.VMEM)
SMEM = pl.BlockSpec(memory_space=pltpu.SMEM)
F32 = jnp.float32
BF16 = jnp.bfloat16


def dot(a, b, dims):
    return lax.dot_general(a, b, ((dims[:1], dims[1:]), ((), ())), preferred_element_type=F32)


def greet(peers):
    barrier = pltpu.get_barrier_semaphore()
    for peer in peers:
        pl.semaphore_signal(barrier, inc=1, device_id=peer, device_id_type=MESH)
    pl.semaphore_wait(barrier, len(peers))


def remote(src, dst, send, recv, index, peer):
    return pltpu.make_async_remote_copy(
        src_ref=src, dst_ref=dst, send_sem=send.at[index], recv_sem=recv.at[index],
        device_id=peer, device_id_type=MESH,
    )


def places(rows):
    row, rep = lax.axis_index("row"), lax.axis_index("rep")
    core = lax.rem(row, 2)
    flip, far = 1 - 2 * core, 6 * core - 3

    def at(shift):
        return (lax.rem(row + shift + rows, rows), rep)

    return flip, far, at


def start_rows(rows, src, band, send, recv, base):
    flip, far, at = places(rows)
    copies = [remote(src, band.at[HOPS - shift], send, recv, base + n, at(shift))
              for n, shift in enumerate((2, -2, far, flip))]
    for copy in copies:
        copy.start()
    return copies


def finish_rows(rows, copies, band, send, recv, base):
    flip, far, at = places(rows)
    passed = []
    for n, shift in enumerate((2, -2)):
        copies[n].wait_recv()
        step = remote(band.at[HOPS - shift], band.at[HOPS - shift - flip], send, recv, base + n, at(flip))
        step.start()
        passed.append(step)
    for copy in copies[2:]:
        copy.wait_recv()
    for copy in copies:
        copy.wait_send()
    for copy in passed:
        copy.wait()


def open_kernel(rows, reps, feats, cot, tiles, cols, band, cots, all_tiles, all_cols, send, recv, local):
    row, rep = lax.axis_index("row"), lax.axis_index("rep")
    flip, far, at = places(rows)
    others = [(row, lax.rem(rep + t, reps)) for t in range(1, reps)]
    greet([at(2), at(-2), at(far), at(flip)] + others)
    copies, n = [], 0
    pieces = ((tiles, all_tiles), (cols, all_cols), (cot, cots))
    pieces = pieces if cot is not None else pieces[:2]
    for peer in others:
        for src, dst in pieces:
            copies.append(remote(src, dst.at[rep], send, recv, n, peer))
            n += 1
    for i, (src, dst) in enumerate(pieces):
        copies.append(pltpu.make_async_copy(src, dst.at[rep], local.at[i]))
    copies.append(pltpu.make_async_copy(feats, band.at[HOPS], local.at[3]))
    for copy in copies:
        copy.start()
    moved = start_rows(rows, feats, band, send, recv, n)
    finish_rows(rows, moved, band, send, recv, n + 4)
    for copy in copies:
        copy.wait()


def scale_terms(rep, reps, cots, w2, dense, degree, terms):
    size = degree.shape[0]
    half = w2.shape[0] // reps
    at = pl.ds(pl.multiple_of(rep * half, half), half)
    pulled = dot(cots[...].reshape(size, -1), w2[at, :], (1, 1))
    scaled = (pulled / degree).astype(BF16)
    scaled_t = scaled.astype(F32).T.astype(BF16)
    for s in range(SPAN):
        part = dot(scaled_t, dense[:, s * size:(s + 1) * size], (1, 0))
        if s == HOPS:
            own = part.T + scaled.astype(F32)
        terms[s] = part.astype(BF16)
    return own


def front_kernel(rows, reps, blocks, tile, tiles, cols, row_ids, band_ids, band,
                 dense, first_o, deg_o):
    row = lax.axis_index("row")
    total = rows * blocks
    per = tiles.shape[2]
    dense[...] = jnp.zeros_like(dense)
    for b in range(blocks):
        at = pl.ds(b * tile, tile)
        ids = row_ids[at, :]
        sums = jnp.ones((tile, 1), F32)
        for j in range(reps):
            for k in range(per):
                slot = lax.rem(cols[j, b, k] + total - (row - HOPS) * blocks, total)
                same = ids == band_ids[pl.ds(slot, 1), :]
                value = jnp.where(same, tiles[j, b, k].astype(F32), 0.0)
                sums = sums + jnp.sum(value, axis=1, keepdims=True)
                dense[at, pl.ds(pl.multiple_of(slot * tile, tile), tile)] = value.astype(BF16)
        deg_o[at, :] = sums
    degree = deg_o[...]
    local = blocks * tile
    flat = band[...].reshape(SPAN * local, -1)
    summed = dot(dense[...], flat, (1, 0))
    first = ((summed + band[HOPS].astype(F32)) / degree).astype(BF16)
    first_o[...] = first


def full_front_kernel(rows, reps, blocks, tile, tiles, cols, row_ids, band_ids, band, cots, w2,
                      dense, first_o, terms_o, own_o, deg_o):
    front_kernel(rows, reps, blocks, tile, tiles, cols, row_ids, band_ids, band, dense, first_o, deg_o)
    own_o[...] = scale_terms(lax.axis_index("rep"), reps, cots, w2, dense, deg_o[...], terms_o)


def band_kernel(rows, first, terms, first_band, term_band, pair, joint, send, recv, local):
    flip, far, at = places(rows)
    greet([at(2), at(-2), at(far), at(flip)])
    joined = [remote(terms.at[HOPS + shift + flip], pair.at[n], send, recv, n, at(flip))
              for n, shift in enumerate((2, -2))]
    for copy in joined:
        copy.start()
    direct = [remote(terms.at[HOPS + far], term_band.at[2], send, recv, 2, at(far))]
    direct[0].start()
    moved = start_rows(rows, first, first_band, send, recv, 3)
    keep = pltpu.make_async_copy(first, first_band.at[HOPS], local.at[0])
    keep.start()
    direct.append(remote(terms.at[HOPS + flip], term_band.at[3], send, recv, 7, at(flip)))
    direct[1].start()
    for n, shift in enumerate((2, -2)):
        joined[n].wait_recv()
        joint[n] = (terms[HOPS + shift].astype(F32) + pair[n].astype(F32)).astype(BF16)
        step = remote(joint.at[n], term_band.at[n], send, recv, 8 + n, at(shift))
        step.start()
        direct.append(step)
    finish_rows(rows, moved, first_band, send, recv, 10)
    keep.wait()
    for copy in joined:
        copy.wait_send()
    for copy in direct:
        copy.wait()


def back_kernel(reps, dense, first_band, term_band, w1, own, deg, cots, second_o, grads_o):
    rep = lax.axis_index("rep")
    local, half = own.shape
    weight = w1[:, pl.ds(pl.multiple_of(rep * half, half), half)]
    preact = dot(first_band[HOPS], weight, (1, 0))
    mine = jnp.maximum(preact, 0.0).astype(BF16)
    summed = mine.astype(F32)
    for s in range(SPAN):
        hidden = mine if s == HOPS else jnp.maximum(dot(first_band[s], weight, (1, 0)), 0.0).astype(BF16)
        summed = summed + dot(dense[:, s * local:(s + 1) * local], hidden, (1, 0))
    second = (summed / deg[...]).astype(BF16)
    second_o[...] = second
    out = dot(second, cots[...].reshape(local, -1), (0, 0))
    width = out.shape[1] // half
    for i in range(width):
        grads_o[i * half:(i + 1) * half, :] = out[:, i * half:(i + 1) * half]
    got = term_band[0].astype(F32)
    for i in range(1, 4):
        got = got + term_band[i].astype(F32)
    back = got.T + own[...]
    delta = jnp.where(preact > 0.0, back, 0.0).astype(BF16)
    grads_o[width * half:, :] = dot(first_band[HOPS], delta, (0, 0))


def swap_kernel(reps, second, full, send, recv, local):
    row, rep = lax.axis_index("row"), lax.axis_index("rep")
    others = [(row, lax.rem(rep + t, reps)) for t in range(1, reps)]
    greet(others)
    copies = [remote(second.at[peer[1]], full.at[rep], send, recv, n, peer) for n, peer in enumerate(others)]
    copies.append(pltpu.make_async_copy(second.at[rep], full.at[rep], local.at[0]))
    for copy in copies:
        copy.start()
    for copy in copies:
        copy.wait()


class Flight:
    def __init__(self, copy):
        self.copy, self.landed, self.left = copy, False, False
        copy.start()

    def wait_send(self):
        if not self.left:
            self.copy.wait_send()
        self.left = True

    def wait_recv(self):
        if not self.landed:
            self.copy.wait_recv()
        self.landed = True

    def wait(self):
        if not self.landed:
            self.copy.wait()
        self.landed = True


def fused_kernel(feats, tiles, cols, sizes, w1, w2, cot, scores_o, whole,
                 band, raw, masked, cots, w1_v, w2_v, cols_v, cols_s, firsts, hidden, terms, deg_v,
                 second_s, second_in, part, paired, total, parcel, parts, send, recv, local):
    row, rep = lax.axis_index("row"), lax.axis_index("rep")
    graphs = sizes.shape[0]
    chip, core = row // 2, lax.rem(row, 2)
    other = 1 - rep
    flip, far, at = places(16)
    mate, sibling = (row, other), at(flip)
    deep, mid, low = chip // 4, lax.rem(chip // 2, 2), lax.rem(chip, 2)
    peers, order = [], []
    for m in range(1, 8):
        q = lax.rem(deep + m // 4, 2) * 4 + lax.rem(mid + m // 2 % 2, 2) * 2 + lax.rem(low + m % 2, 2)
        order.append(q)
        peers.append((q * 2 + core, rep))
    flights, pulls = [], []

    def push(src, dst, peer):
        flights.append(Flight(remote(src, dst, send, recv, len(flights), peer)))
        return flights[-1]

    def pull(src, dst):
        pulls.append(Flight(pltpu.make_async_copy(src, dst, local.at[len(pulls)])))
        return pulls[-1]

    half = pl.ds(pl.multiple_of(rep * 256, 256), 256)
    got_cols = pull(cols, cols_s.at[rep])
    got_tiles = pull(tiles, raw.at[rep])
    got_cot = pull(cot, cots.at[rep])
    got_w2 = pull(w2, w2_v)
    got_w1 = pull(w1.at[:, half], w1_v)
    got_feats = pull(feats, band.at[pl.ds(HOPS * 4, 4)])

    def send_tile(b):
        return push(tiles.at[b], raw.at[rep, b], mate)

    def group(ref, s):
        return ref.at[pl.ds(s * 4, 4)]

    greet(peers + [at(far), sibling, mate])
    came_cols = push(cols, cols_v, mate)
    near = [push(feats, group(band, HOPS - shift), at(shift)) for shift in (2, -2)]
    direct = [push(feats, group(band, HOPS - shift), at(shift)) for shift in (far, flip)]
    came_mine = [send_tile(other * 2 + b) for b in range(2)]

    ends, upto = [], jnp.int32(0)
    for g in range(graphs):
        upto = upto + sizes[g]
        ends.append(upto)

    def graph_of(spots):
        found = jnp.zeros(spots.shape, jnp.int32)
        for end in ends:
            found = found + (spots >= end).astype(jnp.int32)
        return found

    down = lax.broadcasted_iota(jnp.int32, (128, 128), 0)
    along = lax.broadcasted_iota(jnp.int32, (8, 128), 1)
    mine = [rep * 2, rep * 2 + 1]
    theirs = [other * 2, other * 2 + 1]

    def mask(j, b):
        row_ids = graph_of(down + (row * 4 + b) * 128)
        for k in range(4):
            ids = graph_of(along + cols_s[j, b, k] * 128)[:1, :]
            value = jnp.where(row_ids == ids, raw[j, b, k].astype(F32), 0.0).astype(BF16)
            masked[b, pl.ds(pl.multiple_of(j * 512 + k * 128, 128), 128), :] = value.T

    ones = jnp.ones((1024, 128), BF16)

    def count(b):
        deg_v[b] = 1.0 + dot(masked[b], ones, (0, 0))

    def scale(p):
        pulled = dot(cots[p], w2_v[half, :], (1, 1))
        for i in range(2):
            b = p * 2 + i
            scaled = (pulled[i * 128:(i + 1) * 128, :] / jnp.tile(deg_v[b], (1, 2))).astype(BF16)
            value = dot(masked[b], scaled, (1, 0))
            terms[b, :128, :] = (value[:128, :] + scaled.astype(F32)).astype(BF16)
            terms[b, 128:, :] = value[128:, :].astype(BF16)

    def slot_of(b, n):
        return jnp.clip(lax.rem(cols_s[n // 4, b, n % 4] + 64 - (row - HOPS) * 4, 64), 0, 27)

    got_cols.wait()
    got_tiles.wait()
    for b in mine + theirs:
        mask(rep, b)
    came_cols.wait_recv()
    more_cols = pull(cols_v, cols_s.at[other])
    more_cols.wait()
    for copy in came_mine:
        copy.wait_send()
    came_theirs = [send_tile(mine[0]), send_tile(mine[1])]
    for i in range(2):
        came_mine[i].wait_recv()
        mask(other, mine[i])
        count(mine[i])
    passed = []
    for n, shift in enumerate((2, -2)):
        near[n].wait_recv()
        passed.append(push(group(band, HOPS - shift), group(band, HOPS - shift - flip), sibling))
    got_feats.wait()
    for copy in direct + passed:
        copy.wait_recv()
    def span(s, p):
        return firsts.at[pl.ds(s * 4 + p * 2, 2)]

    def offer(p):
        return [push(span(HOPS, p), span(HOPS - shift, p), at(shift)) for shift in (2, -2, far, flip)]

    def smooth(b):
        near_x = jnp.concatenate([band[slot_of(b, n)] for n in range(8)], axis=0)
        value = dot(masked[b], near_x, (0, 0)) + band[HOPS * 4 + b].astype(F32)
        firsts[HOPS * 4 + b] = (value / deg_v[b]).astype(BF16)

    def hide(s):
        x = firsts[s * 4:(s + 1) * 4] if isinstance(s, int) else firsts[pl.ds(s * 4, 4)]
        value = jnp.maximum(dot(x.reshape(512, 128), w1_v[...], (1, 0)), 0.0).astype(BF16)
        hidden[pl.ds(s * 4, 4)] = value.reshape(4, 128, 256)

    for b in mine:
        smooth(b)
    waves = [offer(rep)]
    for copy in came_theirs:
        copy.wait_send()
    came_cot = push(cot, cots.at[rep], mate)
    for i in range(2):
        came_theirs[i].wait_recv()
        mask(other, theirs[i])
        count(theirs[i])
        smooth(theirs[i])
    waves.append(offer(other))
    got_cot.wait()
    got_w2.wait()
    got_w1.wait()
    scale(rep)
    hide(HOPS)
    handed = []
    for p, wave in zip((rep, other), waves):
        for n, shift in enumerate((2, -2)):
            wave[n].wait_recv()
            handed.append(push(span(HOPS - shift, p), span(HOPS - shift - flip, p), sibling))
    for wave in waves:
        wave[2].wait_recv()
        wave[3].wait_recv()
    for s in (HOPS + flip, HOPS - 2, HOPS + 2, HOPS + far):
        hide(s)
    came_cot.wait_recv()
    scale(other)
    for copy in handed:
        copy.wait_recv()
    for shift in (2, -2):
        hide(HOPS - shift + flip)

    for b in range(4):
        near_h = jnp.concatenate([hidden[slot_of(b, n)] for n in range(8)], axis=0)
        value = (dot(masked[b], near_h, (0, 0)) + hidden[HOPS * 4 + b].astype(F32)) / jnp.tile(deg_v[b], (1, 2))
        second_s[b // 2, (b % 2) * 128:(b % 2 + 1) * 128, :] = value.astype(BF16)
        near_f = jnp.concatenate([firsts[slot_of(b, n)] for n in range(8)], axis=0)
        value = dot(near_f, jnp.where(near_h > 0, terms[b], jnp.zeros_like(near_h)), (0, 0))
        gi = value if b == 0 else gi + value
    came_second = push(second_s.at[other], second_in, mate)
    go = dot(second_s[...].reshape(512, 256), cots[...].reshape(512, 512), (0, 0))
    for s in range(16):
        j, q = s // 4, s % 4
        part[s // 8, s % 8, :64, :] = go[q * 64:(q + 1) * 64, j * 128:(j + 1) * 128]
        j, q = s // 8, s % 8
        part[s // 8, s % 8, 64:, :] = gi[q * 16:(q + 1) * 16, j * 128:(j + 1) * 128]
    joined = push(part.at[1 - core], paired, sibling)
    joined.wait_recv()
    total[...] = part[core] + paired[...]
    parcel[...] = total[...].astype(BF16)
    shares = [push(parcel.at[q], parts.at[t], peer) for t, (q, peer) in enumerate(zip(order, peers))]
    came_second.wait_recv()
    scores = dot(second_s[rep], w2_v[half, :], (1, 0))
    scores = scores + dot(second_in[...], w2_v[pl.ds(pl.multiple_of(other * 256, 256), 256), :], (1, 0))
    scores_o[...] = scores.astype(BF16)
    value = total[chip]
    for t, copy in enumerate(shares):
        copy.wait_recv()
        value = value + parts[t].astype(F32)
    whole[rep, core, chip] = value.astype(BF16)

    def spread(p, c, q, peer):
        return push(whole.at[p, c, q], whole.at[p, c, q], peer)

    beyond = [spread(rep, core, chip, mate)]
    rounds = [spread(rep, core, chip, peer) for peer in peers]
    aside = [spread(rep, core, chip, sibling)]
    for t, copy in enumerate(rounds):
        copy.wait_recv()
        beyond.append(spread(rep, core, order[t], mate))
        aside.append(spread(rep, core, order[t], sibling))
    for t, copy in enumerate(beyond):
        copy.wait_recv()
        aside.append(spread(other, core, chip if t == 0 else order[t - 1], sibling))
    for copy in aside:
        copy.wait_recv()
    for flight in flights:
        flight.wait_send()


def end_kernel(scores, whole, scores_o, gi_o, go_o, gi_s, go_s, sem):
    copies = [pltpu.make_async_copy(scores, scores_o, sem.at[0])]
    copies[0].start()
    for p in range(2):
        for s in range(16):
            piece = whole[p, s // 8, s % 8].astype(F32)
            j, q = s // 4, s % 4
            go_s[p * 256 + q * 64:p * 256 + (q + 1) * 64, j * 128:(j + 1) * 128] = piece[:64]
            j, q = s // 8, s % 8
            gi_s[q * 16:(q + 1) * 16, p * 256 + j * 128:p * 256 + (j + 1) * 128] = piece[64:]
        rows = pl.ds(p * 256, 256)
        copies.append(pltpu.make_async_copy(go_s.at[rows], go_o.at[rows], sem.at[1 + p]))
        copies[-1].start()
    copies.append(pltpu.make_async_copy(gi_s, gi_o, sem.at[3]))
    copies[-1].start()
    for copy in copies:
        copy.wait()


def fused(features, input_weight, output_weight, cotangent, adjacency_tiles, block_columns, graph_sizes):
    scores, whole = pl.pallas_call(
        fused_kernel,
        out_shape=(pltpu.VMEM((256, 512), BF16), pltpu.VMEM((2, 2, 8, 80, 128), BF16)),
        in_specs=[HBM, HBM, HBM, SMEM, HBM, HBM, HBM],
        out_specs=(VMEM,) * 2,
        scratch_shapes=[
            pltpu.VMEM((28, 128, 128), BF16),
            pltpu.VMEM((2, 4, 4, 128, 128), BF16),
            pltpu.VMEM((4, 1024, 128), BF16),
            pltpu.VMEM((2, 256, 512), BF16),
            pltpu.VMEM((128, 256), BF16),
            pltpu.VMEM((512, 512), BF16),
            pltpu.VMEM((4, 4), jnp.int32),
            pltpu.SMEM((2, 4, 4), jnp.int32),
            pltpu.VMEM((28, 128, 128), BF16),
            pltpu.VMEM((28, 128, 256), BF16),
            pltpu.VMEM((4, 1024, 256), BF16),
            pltpu.VMEM((4, 128, 128), F32),
            pltpu.VMEM((2, 256, 256), BF16),
            pltpu.VMEM((256, 256), BF16),
            pltpu.VMEM((2, 8, 80, 128), F32),
            pltpu.VMEM((8, 80, 128), F32),
            pltpu.VMEM((8, 80, 128), F32),
            pltpu.VMEM((8, 80, 128), BF16),
            pltpu.VMEM((7, 80, 128), BF16),
            pltpu.SemaphoreType.DMA((72,)),
            pltpu.SemaphoreType.DMA((72,)),
            pltpu.SemaphoreType.DMA((8,)),
        ],
        compiler_params=pltpu.CompilerParams(vmem_limit_bytes=58 << 20, collective_id=0, has_side_effects=True),
    )(features.reshape(4, 128, 128), adjacency_tiles, block_columns, graph_sizes, input_weight, output_weight,
      cotangent)
    return pl.pallas_call(
        end_kernel,
        out_shape=(shape((256, 512), BF16), shape((128, 512), F32), shape((512, 512), F32)),
        in_specs=[VMEM] * 2,
        out_specs=(HBM,) * 3,
        scratch_shapes=[pltpu.VMEM((128, 512), F32), pltpu.VMEM((512, 512), F32), pltpu.SemaphoreType.DMA((4,))],
        compiler_params=params(),
    )(scores, whole)


def params(number=None):
    limit = 48 << 20
    if number is None:
        return pltpu.CompilerParams(vmem_limit_bytes=limit)
    return pltpu.CompilerParams(vmem_limit_bytes=limit, collective_id=number, has_side_effects=True)


def shape(dims, kind):
    return jax.ShapeDtypeStruct(dims, kind)


def sems(count):
    return [pltpu.SemaphoreType.DMA((count,)), pltpu.SemaphoreType.DMA((count,)), pltpu.SemaphoreType.DMA((4,))]


def body(
    features, input_weight, output_weight, cotangent, adjacency_tiles, block_columns, graph_sizes
):
    row = lax.axis_index("row")
    rows, reps = lax.axis_size("row"), lax.axis_size("rep")
    blocks, per, tile = adjacency_tiles.shape[:3]
    local = blocks * tile
    fin = features.shape[1]
    hid = output_weight.shape[0]
    half, quarter = hid // reps, local // reps
    nodes = rows * local
    if (rows, reps, blocks, per) == (16, 2, 4, 4) and graph_sizes.shape[0] <= 32:
        return fused(features, input_weight, output_weight, cotangent, adjacency_tiles, block_columns, graph_sizes)
    upto = jnp.arange(graph_sizes.shape[0])
    ends = jnp.sum(jnp.where(upto[None, :] <= upto[:, None], graph_sizes[None, :], 0), axis=1)

    def graph_of(places):
        return jnp.sum((places[..., None] >= ends).astype(jnp.int32), axis=-1)

    spots = lax.rem((row - HOPS) * local + nodes + jnp.arange(SPAN * local, dtype=jnp.int32), nodes)
    ids = graph_of(spots)
    row_ids = ids[HOPS * local:(HOPS + 1) * local].reshape(local, 1)
    band_ids = ids.reshape(SPAN * blocks, tile)
    padded = jnp.pad(block_columns, ((0, 8 - blocks), (0, 128 - per)))
    tall = hid * hid // reps // half + fin
    band, cots, all_tiles, all_cols = pl.pallas_call(
        functools.partial(open_kernel, rows, reps),
        out_shape=(
            shape((SPAN, local, fin), BF16),
            shape((reps, quarter, hid), BF16),
            shape((reps,) + adjacency_tiles.shape, BF16),
            shape((reps, 8, 128), jnp.int32),
        ),
        in_specs=[HBM] * 4,
        out_specs=(VMEM,) * 3 + (ANY,),
        scratch_shapes=sems(3 * (reps - 1) + 6),
        compiler_params=params(0),
    )(features, cotangent, adjacency_tiles, padded)
    dense, first, terms, own, degree = pl.pallas_call(
        functools.partial(full_front_kernel, rows, reps, blocks, tile),
        out_shape=(
            shape((local, SPAN * local), BF16),
            shape((local, fin), BF16),
            shape((SPAN, half, local), BF16),
            shape((local, half), F32),
            shape((local, 1), F32),
        ),
        in_specs=[VMEM, SMEM] + [VMEM] * 5,
        out_specs=(VMEM,) * 5,
        compiler_params=params(),
    )(all_tiles, all_cols, row_ids, band_ids, band, cots, output_weight)
    first_band, term_band = pl.pallas_call(
        functools.partial(band_kernel, rows),
        out_shape=(shape((SPAN, local, fin), BF16), shape((4, half, local), BF16)),
        in_specs=[VMEM] * 2,
        out_specs=(VMEM,) * 2,
        scratch_shapes=[pltpu.VMEM((2, half, local), BF16)] * 2 + sems(12),
        compiler_params=params(1),
    )(first, terms)
    second, grads = pl.pallas_call(
        functools.partial(back_kernel, reps),
        out_shape=(shape((local, half), BF16), shape((tall, half), F32)),
        in_specs=[VMEM] * 7,
        out_specs=(VMEM,) * 2,
        compiler_params=params(),
    )(dense, first_band, term_band, input_weight, own, degree, cots)
    second = second.reshape(reps, quarter, half)
    full = pl.pallas_call(
        functools.partial(swap_kernel, reps),
        out_shape=shape((reps, quarter, half), BF16),
        in_specs=[ANY],
        out_specs=ANY,
        scratch_shapes=sems(reps),
        compiler_params=params(2),
    )(second)
    whole = lax.all_gather(lax.psum(grads, "row"), "rep", axis=0)
    scores = dot(full.transpose(1, 0, 2).reshape(quarter, hid), output_weight, (1, 0)).astype(BF16)
    grad_input = whole[:, tall - fin:].transpose(1, 0, 2).reshape(fin, hid)
    grad_output = whole[:, :tall - fin].reshape(reps, hid // half, half, half)
    grad_output = grad_output.transpose(0, 2, 1, 3).reshape(hid, hid)
    return scores, grad_input, grad_output


def solution(mesh):
    placed = (
        P("row", None),
        P(),
        P(),
        P(("row", "rep"), None),
        P("row", "rep", None, None),
        P("row", "rep"),
        P(),
    )
    return jax.shard_map(
        body,
        mesh=mesh,
        in_specs=placed,
        out_specs=(P(("row", "rep"), None), P(), P()),
        check_vma=False,
    )
```

```python
import functools

import jax
import jax.numpy as jnp
from jax import lax
from jax.experimental import pallas as pl
from jax.experimental.pallas import tpu as pltpu
from jax.sharding import PartitionSpec as P

HOPS = 3
SPAN = 2 * HOPS + 1
MESH = pl.DeviceIdType.MESH
ANY = pl.BlockSpec(memory_space=pl.ANY)
HBM = pl.BlockSpec(memory_space=pltpu.HBM)
VMEM = pl.BlockSpec(memory_space=pltpu.VMEM)
SMEM = pl.BlockSpec(memory_space=pltpu.SMEM)
F32 = jnp.float32
BF16 = jnp.bfloat16


def dot(a, b, dims):
    return lax.dot_general(a, b, ((dims[:1], dims[1:]), ((), ())), preferred_element_type=F32)


def greet(peers):
    barrier = pltpu.get_barrier_semaphore()
    for peer in peers:
        pl.semaphore_signal(barrier, inc=1, device_id=peer, device_id_type=MESH)
    pl.semaphore_wait(barrier, len(peers))


def remote(src, dst, send, recv, index, peer):
    return pltpu.make_async_remote_copy(
        src_ref=src, dst_ref=dst, send_sem=send.at[index], recv_sem=recv.at[index],
        device_id=peer, device_id_type=MESH,
    )


def places(rows):
    row, rep = lax.axis_index("row"), lax.axis_index("rep")
    core = lax.rem(row, 2)
    flip, far = 1 - 2 * core, 6 * core - 3

    def at(shift):
        return (lax.rem(row + shift + rows, rows), rep)

    return flip, far, at


def start_rows(rows, src, band, send, recv, base):
    flip, far, at = places(rows)
    copies = [remote(src, band.at[HOPS - shift], send, recv, base + n, at(shift))
              for n, shift in enumerate((2, -2, far, flip))]
    for copy in copies:
        copy.start()
    return copies


def finish_rows(rows, copies, band, send, recv, base):
    flip, far, at = places(rows)
    passed = []
    for n, shift in enumerate((2, -2)):
        copies[n].wait_recv()
        step = remote(band.at[HOPS - shift], band.at[HOPS - shift - flip], send, recv, base + n, at(flip))
        step.start()
        passed.append(step)
    for copy in copies[2:]:
        copy.wait_recv()
    for copy in copies:
        copy.wait_send()
    for copy in passed:
        copy.wait()


def open_kernel(rows, reps, feats, cot, tiles, cols, band, cots, all_tiles, all_cols, send, recv, local):
    row, rep = lax.axis_index("row"), lax.axis_index("rep")
    flip, far, at = places(rows)
    others = [(row, lax.rem(rep + t, reps)) for t in range(1, reps)]
    greet([at(2), at(-2), at(far), at(flip)] + others)
    copies, n = [], 0
    pieces = ((tiles, all_tiles), (cols, all_cols), (cot, cots))
    pieces = pieces if cot is not None else pieces[:2]
    for peer in others:
        for src, dst in pieces:
            copies.append(remote(src, dst.at[rep], send, recv, n, peer))
            n += 1
    for i, (src, dst) in enumerate(pieces):
        copies.append(pltpu.make_async_copy(src, dst.at[rep], local.at[i]))
    copies.append(pltpu.make_async_copy(feats, band.at[HOPS], local.at[3]))
    for copy in copies:
        copy.start()
    moved = start_rows(rows, feats, band, send, recv, n)
    finish_rows(rows, moved, band, send, recv, n + 4)
    for copy in copies:
        copy.wait()


def scale_terms(rep, reps, cots, w2, dense, degree, terms):
    size = degree.shape[0]
    half = w2.shape[0] // reps
    at = pl.ds(pl.multiple_of(rep * half, half), half)
    pulled = dot(cots[...].reshape(size, -1), w2[at, :], (1, 1))
    scaled = (pulled / degree).astype(BF16)
    scaled_t = scaled.astype(F32).T.astype(BF16)
    for s in range(SPAN):
        part = dot(scaled_t, dense[:, s * size:(s + 1) * size], (1, 0))
        if s == HOPS:
            own = part.T + scaled.astype(F32)
        terms[s] = part.astype(BF16)
    return own


def front_kernel(rows, reps, blocks, tile, tiles, cols, row_ids, band_ids, band,
                 dense, first_o, deg_o):
    row = lax.axis_index("row")
    total = rows * blocks
    per = tiles.shape[2]
    dense[...] = jnp.zeros_like(dense)
    for b in range(blocks):
        at = pl.ds(b * tile, tile)
        ids = row_ids[at, :]
        sums = jnp.ones((tile, 1), F32)
        for j in range(reps):
            for k in range(per):
                slot = lax.rem(cols[j, b, k] + total - (row - HOPS) * blocks, total)
                same = ids == band_ids[pl.ds(slot, 1), :]
                value = jnp.where(same, tiles[j, b, k].astype(F32), 0.0)
                sums = sums + jnp.sum(value, axis=1, keepdims=True)
                dense[at, pl.ds(pl.multiple_of(slot * tile, tile), tile)] = value.astype(BF16)
        deg_o[at, :] = sums
    degree = deg_o[...]
    local = blocks * tile
    flat = band[...].reshape(SPAN * local, -1)
    summed = dot(dense[...], flat, (1, 0))
    first = ((summed + band[HOPS].astype(F32)) / degree).astype(BF16)
    first_o[...] = first


def full_front_kernel(rows, reps, blocks, tile, tiles, cols, row_ids, band_ids, band, cots, w2,
                      dense, first_o, terms_o, own_o, deg_o):
    front_kernel(rows, reps, blocks, tile, tiles, cols, row_ids, band_ids, band, dense, first_o, deg_o)
    own_o[...] = scale_terms(lax.axis_index("rep"), reps, cots, w2, dense, deg_o[...], terms_o)


def band_kernel(rows, first, terms, first_band, term_band, pair, joint, send, recv, local):
    flip, far, at = places(rows)
    greet([at(2), at(-2), at(far), at(flip)])
    joined = [remote(terms.at[HOPS + shift + flip], pair.at[n], send, recv, n, at(flip))
              for n, shift in enumerate((2, -2))]
    for copy in joined:
        copy.start()
    direct = [remote(terms.at[HOPS + far], term_band.at[2], send, recv, 2, at(far))]
    direct[0].start()
    moved = start_rows(rows, first, first_band, send, recv, 3)
    keep = pltpu.make_async_copy(first, first_band.at[HOPS], local.at[0])
    keep.start()
    direct.append(remote(terms.at[HOPS + flip], term_band.at[3], send, recv, 7, at(flip)))
    direct[1].start()
    for n, shift in enumerate((2, -2)):
        joined[n].wait_recv()
        joint[n] = (terms[HOPS + shift].astype(F32) + pair[n].astype(F32)).astype(BF16)
        step = remote(joint.at[n], term_band.at[n], send, recv, 8 + n, at(shift))
        step.start()
        direct.append(step)
    finish_rows(rows, moved, first_band, send, recv, 10)
    keep.wait()
    for copy in joined:
        copy.wait_send()
    for copy in direct:
        copy.wait()


def back_kernel(reps, dense, first_band, term_band, w1, own, deg, cots, second_o, grads_o):
    rep = lax.axis_index("rep")
    local, half = own.shape
    weight = w1[:, pl.ds(pl.multiple_of(rep * half, half), half)]
    preact = dot(first_band[HOPS], weight, (1, 0))
    mine = jnp.maximum(preact, 0.0).astype(BF16)
    summed = mine.astype(F32)
    for s in range(SPAN):
        hidden = mine if s == HOPS else jnp.maximum(dot(first_band[s], weight, (1, 0)), 0.0).astype(BF16)
        summed = summed + dot(dense[:, s * local:(s + 1) * local], hidden, (1, 0))
    second = (summed / deg[...]).astype(BF16)
    second_o[...] = second
    out = dot(second, cots[...].reshape(local, -1), (0, 0))
    width = out.shape[1] // half
    for i in range(width):
        grads_o[i * half:(i + 1) * half, :] = out[:, i * half:(i + 1) * half]
    got = term_band[0].astype(F32)
    for i in range(1, 4):
        got = got + term_band[i].astype(F32)
    back = got.T + own[...]
    delta = jnp.where(preact > 0.0, back, 0.0).astype(BF16)
    grads_o[width * half:, :] = dot(first_band[HOPS], delta, (0, 0))


def swap_kernel(reps, second, full, send, recv, local):
    row, rep = lax.axis_index("row"), lax.axis_index("rep")
    others = [(row, lax.rem(rep + t, reps)) for t in range(1, reps)]
    greet(others)
    copies = [remote(second.at[peer[1]], full.at[rep], send, recv, n, peer) for n, peer in enumerate(others)]
    copies.append(pltpu.make_async_copy(second.at[rep], full.at[rep], local.at[0]))
    for copy in copies:
        copy.start()
    for copy in copies:
        copy.wait()


class Flight:
    def __init__(self, copy):
        self.copy, self.landed, self.left = copy, False, False
        copy.start()

    def wait_send(self):
        if not self.left:
            self.copy.wait_send()
        self.left = True

    def wait_recv(self):
        if not self.landed:
            self.copy.wait_recv()
        self.landed = True

    def wait(self):
        if not self.landed:
            self.copy.wait()
        self.landed = True


def fused_kernel(feats, tiles, cols, sizes, w1, w2, cot, scores_o, whole,
                 band, raw, masked, cots, w1_v, w2_v, cols_v, cols_s, firsts, hidden, terms, deg_v,
                 second_s, second_in, part, paired, total, parcel, parts, send, recv, local):
    row, rep = lax.axis_index("row"), lax.axis_index("rep")
    graphs = sizes.shape[0]
    chip, core = row // 2, lax.rem(row, 2)
    other = 1 - rep
    flip, far, at = places(16)
    mate, sibling = (row, other), at(flip)
    deep, mid, low = chip // 4, lax.rem(chip // 2, 2), lax.rem(chip, 2)
    peers, order = [], []
    for m in range(1, 8):
        q = lax.rem(deep + m // 4, 2) * 4 + lax.rem(mid + m // 2 % 2, 2) * 2 + lax.rem(low + m % 2, 2)
        order.append(q)
        peers.append((q * 2 + core, rep))
    flights, pulls = [], []

    def push(src, dst, peer):
        flights.append(Flight(remote(src, dst, send, recv, len(flights), peer)))
        return flights[-1]

    def pull(src, dst):
        pulls.append(Flight(pltpu.make_async_copy(src, dst, local.at[len(pulls)])))
        return pulls[-1]

    half = pl.ds(pl.multiple_of(rep * 256, 256), 256)
    got_cols = pull(cols, cols_s.at[rep])
    got_tiles = pull(tiles, raw.at[rep])
    got_cot = pull(cot, cots.at[rep])
    got_w2 = pull(w2, w2_v)
    got_w1 = pull(w1.at[:, half], w1_v)
    got_feats = pull(feats, band.at[pl.ds(HOPS * 4, 4)])

    def send_tile(b):
        return push(tiles.at[b], raw.at[rep, b], mate)

    def group(ref, s):
        return ref.at[pl.ds(s * 4, 4)]

    greet(peers + [at(far), sibling, mate])
    came_cols = push(cols, cols_v, mate)
    near = [push(feats, group(band, HOPS - shift), at(shift)) for shift in (2, -2)]
    direct = [push(feats, group(band, HOPS - shift), at(shift)) for shift in (far, flip)]
    came_mine = [send_tile(other * 2 + b) for b in range(2)]

    ends, upto = [], jnp.int32(0)
    for g in range(graphs):
        upto = upto + sizes[g]
        ends.append(upto)

    def graph_of(spots):
        found = jnp.zeros(spots.shape, jnp.int32)
        for end in ends:
            found = found + (spots >= end).astype(jnp.int32)
        return found

    down = lax.broadcasted_iota(jnp.int32, (128, 128), 0)
    along = lax.broadcasted_iota(jnp.int32, (8, 128), 1)
    mine = [rep * 2, rep * 2 + 1]
    theirs = [other * 2, other * 2 + 1]

    def mask(j, b):
        row_ids = graph_of(down + (row * 4 + b) * 128)
        for k in range(4):
            ids = graph_of(along + cols_s[j, b, k] * 128)[:1, :]
            value = jnp.where(row_ids == ids, raw[j, b, k].astype(F32), 0.0).astype(BF16)
            masked[b, pl.ds(pl.multiple_of(j * 512 + k * 128, 128), 128), :] = value.T

    ones = jnp.ones((1024, 128), BF16)

    def count(b):
        deg_v[b] = 1.0 + dot(masked[b], ones, (0, 0))

    def scale(p):
        pulled = dot(cots[p], w2_v[half, :], (1, 1))
        for i in range(2):
            b = p * 2 + i
            scaled = (pulled[i * 128:(i + 1) * 128, :] / jnp.tile(deg_v[b], (1, 2))).astype(BF16)
            value = dot(masked[b], scaled, (1, 0))
            terms[b, :128, :] = (value[:128, :] + scaled.astype(F32)).astype(BF16)
            terms[b, 128:, :] = value[128:, :].astype(BF16)

    def slot_of(b, n):
        return jnp.clip(lax.rem(cols_s[n // 4, b, n % 4] + 64 - (row - HOPS) * 4, 64), 0, 27)

    got_cols.wait()
    got_tiles.wait()
    for b in mine + theirs:
        mask(rep, b)
    came_cols.wait_recv()
    more_cols = pull(cols_v, cols_s.at[other])
    more_cols.wait()
    for copy in came_mine:
        copy.wait_send()
    came_theirs = [send_tile(mine[0]), send_tile(mine[1])]
    for i in range(2):
        came_mine[i].wait_recv()
        mask(other, mine[i])
        count(mine[i])
    passed = []
    for n, shift in enumerate((2, -2)):
        near[n].wait_recv()
        passed.append(push(group(band, HOPS - shift), group(band, HOPS - shift - flip), sibling))
    got_feats.wait()
    for copy in direct + passed:
        copy.wait_recv()
    def span(s, p):
        return firsts.at[pl.ds(s * 4 + p * 2, 2)]

    def offer(p):
        return [push(span(HOPS, p), span(HOPS - shift, p), at(shift)) for shift in (2, -2, far, flip)]

    def smooth(b):
        near_x = jnp.concatenate([band[slot_of(b, n)] for n in range(8)], axis=0)
        value = dot(masked[b], near_x, (0, 0)) + band[HOPS * 4 + b].astype(F32)
        firsts[HOPS * 4 + b] = (value / deg_v[b]).astype(BF16)

    def hide(s):
        x = firsts[s * 4:(s + 1) * 4] if isinstance(s, int) else firsts[pl.ds(s * 4, 4)]
        value = jnp.maximum(dot(x.reshape(512, 128), w1_v[...], (1, 0)), 0.0).astype(BF16)
        hidden[pl.ds(s * 4, 4)] = value.reshape(4, 128, 256)

    for b in mine:
        smooth(b)
    waves = [offer(rep)]
    for copy in came_theirs:
        copy.wait_send()
    came_cot = push(cot, cots.at[rep], mate)
    for i in range(2):
        came_theirs[i].wait_recv()
        mask(other, theirs[i])
        count(theirs[i])
        smooth(theirs[i])
    waves.append(offer(other))
    got_cot.wait()
    got_w2.wait()
    got_w1.wait()
    scale(rep)
    hide(HOPS)
    handed = []
    for p, wave in zip((rep, other), waves):
        for n, shift in enumerate((2, -2)):
            wave[n].wait_recv()
            handed.append(push(span(HOPS - shift, p), span(HOPS - shift - flip, p), sibling))
    for wave in waves:
        wave[2].wait_recv()
        wave[3].wait_recv()
    for s in (HOPS + flip, HOPS - 2, HOPS + 2, HOPS + far):
        hide(s)
    came_cot.wait_recv()
    scale(other)
    for copy in handed:
        copy.wait_recv()
    for shift in (2, -2):
        hide(HOPS - shift + flip)

    for b in range(4):
        near_h = jnp.concatenate([hidden[slot_of(b, n)] for n in range(8)], axis=0)
        value = (dot(masked[b], near_h, (0, 0)) + hidden[HOPS * 4 + b].astype(F32)) / jnp.tile(deg_v[b], (1, 2))
        second_s[b // 2, (b % 2) * 128:(b % 2 + 1) * 128, :] = value.astype(BF16)
        near_f = jnp.concatenate([firsts[slot_of(b, n)] for n in range(8)], axis=0)
        value = dot(near_f, jnp.where(near_h > 0, terms[b], jnp.zeros_like(near_h)), (0, 0))
        gi = value if b == 0 else gi + value
    came_second = push(second_s.at[other], second_in, mate)
    for s in range(16):
        j, q = s // 8, s % 8
        part[s // 8, s % 8, 64:, :] = gi[q * 16:(q + 1) * 16, j * 128:(j + 1) * 128]

    def outer(c):
        lanes = pl.ds(pl.multiple_of(c * 256, 256), 256)
        go = dot(second_s[...].reshape(512, 256), cots[:, :, lanes].reshape(512, 256), (0, 0))
        for s in range(8):
            j, q = s // 4, s % 4
            part[c, s, :64, :] = go[q * 64:(q + 1) * 64, j * 128:(j + 1) * 128]

    outer(1 - core)
    joined = push(part.at[1 - core], paired, sibling)
    outer(core)
    joined.wait_recv()
    shares = []
    for q, peer in zip(order, peers):
        parcel[q] = (part[core, q] + paired[q]).astype(BF16)
        shares.append(push(parcel.at[q], parts.at[len(shares)], peer))
    total[...] = part[core, chip] + paired[chip]
    came_second.wait_recv()
    scores = dot(second_s[rep], w2_v[half, :], (1, 0))
    scores = scores + dot(second_in[...], w2_v[pl.ds(pl.multiple_of(other * 256, 256), 256), :], (1, 0))
    scores_o[...] = scores.astype(BF16)
    value = total[...]
    for t, copy in enumerate(shares):
        copy.wait_recv()
        value = value + parts[t].astype(F32)
    whole[rep, core, chip] = value.astype(BF16)

    def spread(p, c, q, peer):
        return push(whole.at[p, c, q], whole.at[p, c, q], peer)

    beyond = [spread(rep, core, chip, mate)]
    rounds = [spread(rep, core, chip, peer) for peer in peers]
    aside = [spread(rep, core, chip, sibling)]
    for t, copy in enumerate(rounds):
        copy.wait_recv()
        beyond.append(spread(rep, core, order[t], mate))
        aside.append(spread(rep, core, order[t], sibling))
    for t, copy in enumerate(beyond):
        copy.wait_recv()
        aside.append(spread(other, core, chip if t == 0 else order[t - 1], sibling))
    for copy in aside:
        copy.wait_recv()
    for flight in flights:
        flight.wait_send()


def end_kernel(scores, whole, scores_o, gi_o, go_o, gi_s, go_s, sem):
    copies = [pltpu.make_async_copy(scores, scores_o, sem.at[0])]
    copies[0].start()
    for p in range(2):
        for s in range(16):
            piece = whole[p, s // 8, s % 8].astype(F32)
            j, q = s // 4, s % 4
            go_s[p * 256 + q * 64:p * 256 + (q + 1) * 64, j * 128:(j + 1) * 128] = piece[:64]
            j, q = s // 8, s % 8
            gi_s[q * 16:(q + 1) * 16, p * 256 + j * 128:p * 256 + (j + 1) * 128] = piece[64:]
        rows = pl.ds(p * 256, 256)
        copies.append(pltpu.make_async_copy(go_s.at[rows], go_o.at[rows], sem.at[1 + p]))
        copies[-1].start()
    copies.append(pltpu.make_async_copy(gi_s, gi_o, sem.at[3]))
    copies[-1].start()
    for copy in copies:
        copy.wait()


def fused(features, input_weight, output_weight, cotangent, adjacency_tiles, block_columns, graph_sizes):
    scores, whole = pl.pallas_call(
        fused_kernel,
        out_shape=(pltpu.VMEM((256, 512), BF16), pltpu.VMEM((2, 2, 8, 80, 128), BF16)),
        in_specs=[HBM, HBM, HBM, SMEM, HBM, HBM, HBM],
        out_specs=(VMEM,) * 2,
        scratch_shapes=[
            pltpu.VMEM((28, 128, 128), BF16),
            pltpu.VMEM((2, 4, 4, 128, 128), BF16),
            pltpu.VMEM((4, 1024, 128), BF16),
            pltpu.VMEM((2, 256, 512), BF16),
            pltpu.VMEM((128, 256), BF16),
            pltpu.VMEM((512, 512), BF16),
            pltpu.VMEM((4, 4), jnp.int32),
            pltpu.SMEM((2, 4, 4), jnp.int32),
            pltpu.VMEM((28, 128, 128), BF16),
            pltpu.VMEM((28, 128, 256), BF16),
            pltpu.VMEM((4, 1024, 256), BF16),
            pltpu.VMEM((4, 128, 128), F32),
            pltpu.VMEM((2, 256, 256), BF16),
            pltpu.VMEM((256, 256), BF16),
            pltpu.VMEM((2, 8, 80, 128), F32),
            pltpu.VMEM((8, 80, 128), F32),
            pltpu.VMEM((80, 128), F32),
            pltpu.VMEM((8, 80, 128), BF16),
            pltpu.VMEM((7, 80, 128), BF16),
            pltpu.SemaphoreType.DMA((72,)),
            pltpu.SemaphoreType.DMA((72,)),
            pltpu.SemaphoreType.DMA((8,)),
        ],
        compiler_params=pltpu.CompilerParams(vmem_limit_bytes=58 << 20, collective_id=0, has_side_effects=True),
    )(features.reshape(4, 128, 128), adjacency_tiles, block_columns, graph_sizes, input_weight, output_weight,
      cotangent)
    return pl.pallas_call(
        end_kernel,
        out_shape=(shape((256, 512), BF16), shape((128, 512), F32), shape((512, 512), F32)),
        in_specs=[VMEM] * 2,
        out_specs=(HBM,) * 3,
        scratch_shapes=[pltpu.VMEM((128, 512), F32), pltpu.VMEM((512, 512), F32), pltpu.SemaphoreType.DMA((4,))],
        compiler_params=params(),
    )(scores, whole)


def params(number=None):
    limit = 48 << 20
    if number is None:
        return pltpu.CompilerParams(vmem_limit_bytes=limit)
    return pltpu.CompilerParams(vmem_limit_bytes=limit, collective_id=number, has_side_effects=True)


def shape(dims, kind):
    return jax.ShapeDtypeStruct(dims, kind)


def sems(count):
    return [pltpu.SemaphoreType.DMA((count,)), pltpu.SemaphoreType.DMA((count,)), pltpu.SemaphoreType.DMA((4,))]


def body(
    features, input_weight, output_weight, cotangent, adjacency_tiles, block_columns, graph_sizes
):
    row = lax.axis_index("row")
    rows, reps = lax.axis_size("row"), lax.axis_size("rep")
    blocks, per, tile = adjacency_tiles.shape[:3]
    local = blocks * tile
    fin = features.shape[1]
    hid = output_weight.shape[0]
    half, quarter = hid // reps, local // reps
    nodes = rows * local
    if (rows, reps, blocks, per) == (16, 2, 4, 4) and graph_sizes.shape[0] <= 32:
        return fused(features, input_weight, output_weight, cotangent, adjacency_tiles, block_columns, graph_sizes)
    upto = jnp.arange(graph_sizes.shape[0])
    ends = jnp.sum(jnp.where(upto[None, :] <= upto[:, None], graph_sizes[None, :], 0), axis=1)

    def graph_of(places):
        return jnp.sum((places[..., None] >= ends).astype(jnp.int32), axis=-1)

    spots = lax.rem((row - HOPS) * local + nodes + jnp.arange(SPAN * local, dtype=jnp.int32), nodes)
    ids = graph_of(spots)
    row_ids = ids[HOPS * local:(HOPS + 1) * local].reshape(local, 1)
    band_ids = ids.reshape(SPAN * blocks, tile)
    padded = jnp.pad(block_columns, ((0, 8 - blocks), (0, 128 - per)))
    tall = hid * hid // reps // half + fin
    band, cots, all_tiles, all_cols = pl.pallas_call(
        functools.partial(open_kernel, rows, reps),
        out_shape=(
            shape((SPAN, local, fin), BF16),
            shape((reps, quarter, hid), BF16),
            shape((reps,) + adjacency_tiles.shape, BF16),
            shape((reps, 8, 128), jnp.int32),
        ),
        in_specs=[HBM] * 4,
        out_specs=(VMEM,) * 3 + (ANY,),
        scratch_shapes=sems(3 * (reps - 1) + 6),
        compiler_params=params(0),
    )(features, cotangent, adjacency_tiles, padded)
    dense, first, terms, own, degree = pl.pallas_call(
        functools.partial(full_front_kernel, rows, reps, blocks, tile),
        out_shape=(
            shape((local, SPAN * local), BF16),
            shape((local, fin), BF16),
            shape((SPAN, half, local), BF16),
            shape((local, half), F32),
            shape((local, 1), F32),
        ),
        in_specs=[VMEM, SMEM] + [VMEM] * 5,
        out_specs=(VMEM,) * 5,
        compiler_params=params(),
    )(all_tiles, all_cols, row_ids, band_ids, band, cots, output_weight)
    first_band, term_band = pl.pallas_call(
        functools.partial(band_kernel, rows),
        out_shape=(shape((SPAN, local, fin), BF16), shape((4, half, local), BF16)),
        in_specs=[VMEM] * 2,
        out_specs=(VMEM,) * 2,
        scratch_shapes=[pltpu.VMEM((2, half, local), BF16)] * 2 + sems(12),
        compiler_params=params(1),
    )(first, terms)
    second, grads = pl.pallas_call(
        functools.partial(back_kernel, reps),
        out_shape=(shape((local, half), BF16), shape((tall, half), F32)),
        in_specs=[VMEM] * 7,
        out_specs=(VMEM,) * 2,
        compiler_params=params(),
    )(dense, first_band, term_band, input_weight, own, degree, cots)
    second = second.reshape(reps, quarter, half)
    full = pl.pallas_call(
        functools.partial(swap_kernel, reps),
        out_shape=shape((reps, quarter, half), BF16),
        in_specs=[ANY],
        out_specs=ANY,
        scratch_shapes=sems(reps),
        compiler_params=params(2),
    )(second)
    whole = lax.all_gather(lax.psum(grads, "row"), "rep", axis=0)
    scores = dot(full.transpose(1, 0, 2).reshape(quarter, hid), output_weight, (1, 0)).astype(BF16)
    grad_input = whole[:, tall - fin:].transpose(1, 0, 2).reshape(fin, hid)
    grad_output = whole[:, :tall - fin].reshape(reps, hid // half, half, half)
    grad_output = grad_output.transpose(0, 2, 1, 3).reshape(hid, hid)
    return scores, grad_input, grad_output


def solution(mesh):
    placed = (
        P("row", None),
        P(),
        P(),
        P(("row", "rep"), None),
        P("row", "rep", None, None),
        P("row", "rep"),
        P(),
    )
    return jax.shard_map(
        body,
        mesh=mesh,
        in_specs=placed,
        out_specs=(P(("row", "rep"), None), P(), P()),
        check_vma=False,
    )
```

```python
import functools

import jax
import jax.numpy as jnp
from jax import lax
from jax.experimental import pallas as pl
from jax.experimental.pallas import tpu as pltpu
from jax.sharding import PartitionSpec as P

HOPS = 3
SPAN = 2 * HOPS + 1
MESH = pl.DeviceIdType.MESH
ANY = pl.BlockSpec(memory_space=pl.ANY)
HBM = pl.BlockSpec(memory_space=pltpu.HBM)
VMEM = pl.BlockSpec(memory_space=pltpu.VMEM)
SMEM = pl.BlockSpec(memory_space=pltpu.SMEM)
F32 = jnp.float32
BF16 = jnp.bfloat16


def dot(a, b, dims):
    return lax.dot_general(a, b, ((dims[:1], dims[1:]), ((), ())), preferred_element_type=F32)


def greet(peers):
    barrier = pltpu.get_barrier_semaphore()
    for peer in peers:
        pl.semaphore_signal(barrier, inc=1, device_id=peer, device_id_type=MESH)
    pl.semaphore_wait(barrier, len(peers))


def remote(src, dst, send, recv, index, peer):
    return pltpu.make_async_remote_copy(
        src_ref=src, dst_ref=dst, send_sem=send.at[index], recv_sem=recv.at[index],
        device_id=peer, device_id_type=MESH,
    )


def places(rows):
    row, rep = lax.axis_index("row"), lax.axis_index("rep")
    core = lax.rem(row, 2)
    flip, far = 1 - 2 * core, 6 * core - 3

    def at(shift):
        return (lax.rem(row + shift + rows, rows), rep)

    return flip, far, at


def start_rows(rows, src, band, send, recv, base):
    flip, far, at = places(rows)
    copies = [remote(src, band.at[HOPS - shift], send, recv, base + n, at(shift))
              for n, shift in enumerate((2, -2, far, flip))]
    for copy in copies:
        copy.start()
    return copies


def finish_rows(rows, copies, band, send, recv, base):
    flip, far, at = places(rows)
    passed = []
    for n, shift in enumerate((2, -2)):
        copies[n].wait_recv()
        step = remote(band.at[HOPS - shift], band.at[HOPS - shift - flip], send, recv, base + n, at(flip))
        step.start()
        passed.append(step)
    for copy in copies[2:]:
        copy.wait_recv()
    for copy in copies:
        copy.wait_send()
    for copy in passed:
        copy.wait()


def open_kernel(rows, reps, feats, cot, tiles, cols, band, cots, all_tiles, all_cols, send, recv, local):
    row, rep = lax.axis_index("row"), lax.axis_index("rep")
    flip, far, at = places(rows)
    others = [(row, lax.rem(rep + t, reps)) for t in range(1, reps)]
    greet([at(2), at(-2), at(far), at(flip)] + others)
    copies, n = [], 0
    pieces = ((tiles, all_tiles), (cols, all_cols), (cot, cots))
    pieces = pieces if cot is not None else pieces[:2]
    for peer in others:
        for src, dst in pieces:
            copies.append(remote(src, dst.at[rep], send, recv, n, peer))
            n += 1
    for i, (src, dst) in enumerate(pieces):
        copies.append(pltpu.make_async_copy(src, dst.at[rep], local.at[i]))
    copies.append(pltpu.make_async_copy(feats, band.at[HOPS], local.at[3]))
    for copy in copies:
        copy.start()
    moved = start_rows(rows, feats, band, send, recv, n)
    finish_rows(rows, moved, band, send, recv, n + 4)
    for copy in copies:
        copy.wait()


def scale_terms(rep, reps, cots, w2, dense, degree, terms):
    size = degree.shape[0]
    half = w2.shape[0] // reps
    at = pl.ds(pl.multiple_of(rep * half, half), half)
    pulled = dot(cots[...].reshape(size, -1), w2[at, :], (1, 1))
    scaled = (pulled / degree).astype(BF16)
    scaled_t = scaled.astype(F32).T.astype(BF16)
    for s in range(SPAN):
        part = dot(scaled_t, dense[:, s * size:(s + 1) * size], (1, 0))
        if s == HOPS:
            own = part.T + scaled.astype(F32)
        terms[s] = part.astype(BF16)
    return own


def front_kernel(rows, reps, blocks, tile, tiles, cols, row_ids, band_ids, band,
                 dense, first_o, deg_o):
    row = lax.axis_index("row")
    total = rows * blocks
    per = tiles.shape[2]
    dense[...] = jnp.zeros_like(dense)
    for b in range(blocks):
        at = pl.ds(b * tile, tile)
        ids = row_ids[at, :]
        sums = jnp.ones((tile, 1), F32)
        for j in range(reps):
            for k in range(per):
                slot = lax.rem(cols[j, b, k] + total - (row - HOPS) * blocks, total)
                same = ids == band_ids[pl.ds(slot, 1), :]
                value = jnp.where(same, tiles[j, b, k].astype(F32), 0.0)
                sums = sums + jnp.sum(value, axis=1, keepdims=True)
                dense[at, pl.ds(pl.multiple_of(slot * tile, tile), tile)] = value.astype(BF16)
        deg_o[at, :] = sums
    degree = deg_o[...]
    local = blocks * tile
    flat = band[...].reshape(SPAN * local, -1)
    summed = dot(dense[...], flat, (1, 0))
    first = ((summed + band[HOPS].astype(F32)) / degree).astype(BF16)
    first_o[...] = first


def full_front_kernel(rows, reps, blocks, tile, tiles, cols, row_ids, band_ids, band, cots, w2,
                      dense, first_o, terms_o, own_o, deg_o):
    front_kernel(rows, reps, blocks, tile, tiles, cols, row_ids, band_ids, band, dense, first_o, deg_o)
    own_o[...] = scale_terms(lax.axis_index("rep"), reps, cots, w2, dense, deg_o[...], terms_o)


def band_kernel(rows, first, terms, first_band, term_band, pair, joint, send, recv, local):
    flip, far, at = places(rows)
    greet([at(2), at(-2), at(far), at(flip)])
    joined = [remote(terms.at[HOPS + shift + flip], pair.at[n], send, recv, n, at(flip))
              for n, shift in enumerate((2, -2))]
    for copy in joined:
        copy.start()
    direct = [remote(terms.at[HOPS + far], term_band.at[2], send, recv, 2, at(far))]
    direct[0].start()
    moved = start_rows(rows, first, first_band, send, recv, 3)
    keep = pltpu.make_async_copy(first, first_band.at[HOPS], local.at[0])
    keep.start()
    direct.append(remote(terms.at[HOPS + flip], term_band.at[3], send, recv, 7, at(flip)))
    direct[1].start()
    for n, shift in enumerate((2, -2)):
        joined[n].wait_recv()
        joint[n] = (terms[HOPS + shift].astype(F32) + pair[n].astype(F32)).astype(BF16)
        step = remote(joint.at[n], term_band.at[n], send, recv, 8 + n, at(shift))
        step.start()
        direct.append(step)
    finish_rows(rows, moved, first_band, send, recv, 10)
    keep.wait()
    for copy in joined:
        copy.wait_send()
    for copy in direct:
        copy.wait()


def back_kernel(reps, dense, first_band, term_band, w1, own, deg, cots, second_o, grads_o):
    rep = lax.axis_index("rep")
    local, half = own.shape
    weight = w1[:, pl.ds(pl.multiple_of(rep * half, half), half)]
    preact = dot(first_band[HOPS], weight, (1, 0))
    mine = jnp.maximum(preact, 0.0).astype(BF16)
    summed = mine.astype(F32)
    for s in range(SPAN):
        hidden = mine if s == HOPS else jnp.maximum(dot(first_band[s], weight, (1, 0)), 0.0).astype(BF16)
        summed = summed + dot(dense[:, s * local:(s + 1) * local], hidden, (1, 0))
    second = (summed / deg[...]).astype(BF16)
    second_o[...] = second
    out = dot(second, cots[...].reshape(local, -1), (0, 0))
    width = out.shape[1] // half
    for i in range(width):
        grads_o[i * half:(i + 1) * half, :] = out[:, i * half:(i + 1) * half]
    got = term_band[0].astype(F32)
    for i in range(1, 4):
        got = got + term_band[i].astype(F32)
    back = got.T + own[...]
    delta = jnp.where(preact > 0.0, back, 0.0).astype(BF16)
    grads_o[width * half:, :] = dot(first_band[HOPS], delta, (0, 0))


def swap_kernel(reps, second, full, send, recv, local):
    row, rep = lax.axis_index("row"), lax.axis_index("rep")
    others = [(row, lax.rem(rep + t, reps)) for t in range(1, reps)]
    greet(others)
    copies = [remote(second.at[peer[1]], full.at[rep], send, recv, n, peer) for n, peer in enumerate(others)]
    copies.append(pltpu.make_async_copy(second.at[rep], full.at[rep], local.at[0]))
    for copy in copies:
        copy.start()
    for copy in copies:
        copy.wait()


class Flight:
    def __init__(self, copy):
        self.copy, self.landed, self.left = copy, False, False
        copy.start()

    def wait_send(self):
        if not self.left:
            self.copy.wait_send()
        self.left = True

    def wait_recv(self):
        if not self.landed:
            self.copy.wait_recv()
        self.landed = True

    def wait(self):
        if not self.landed:
            self.copy.wait()
        self.landed = True


def fused_kernel(feats, tiles, cols, sizes, w1, w2, cot, scores_o, whole,
                 band, raw, masked, cots, w1_v, w2_v, cols_v, cols_s, firsts, hidden, terms, deg_v,
                 second_s, second_in, part, paired, total, parcel, parts, send, recv, local):
    row, rep = lax.axis_index("row"), lax.axis_index("rep")
    graphs = sizes.shape[0]
    chip, core = row // 2, lax.rem(row, 2)
    other = 1 - rep
    flip, far, at = places(16)
    mate, sibling = (row, other), at(flip)
    deep, mid, low = chip // 4, lax.rem(chip // 2, 2), lax.rem(chip, 2)
    peers, order = [], []
    for m in range(1, 8):
        q = lax.rem(deep + m // 4, 2) * 4 + lax.rem(mid + m // 2 % 2, 2) * 2 + lax.rem(low + m % 2, 2)
        order.append(q)
        peers.append((q * 2 + core, rep))
    flights, pulls = [], []

    def push(src, dst, peer):
        flights.append(Flight(remote(src, dst, send, recv, len(flights), peer)))
        return flights[-1]

    def pull(src, dst):
        pulls.append(Flight(pltpu.make_async_copy(src, dst, local.at[len(pulls)])))
        return pulls[-1]

    half = pl.ds(pl.multiple_of(rep * 256, 256), 256)
    got_cols = pull(cols, cols_s.at[rep])
    got_tiles = pull(tiles, raw.at[rep])
    got_cot = pull(cot, cots.at[rep])
    got_w2 = pull(w2, w2_v)
    got_w1 = pull(w1.at[:, half], w1_v)
    got_feats = pull(feats, band.at[pl.ds(HOPS * 4, 4)])

    def send_tile(b):
        return push(tiles.at[b], raw.at[rep, b], mate)

    def group(ref, s):
        return ref.at[pl.ds(s * 4, 4)]

    greet(peers[::-1] + [at(far), mate, sibling])
    came_cols = push(cols, cols_v, mate)
    near = [push(feats, group(band, HOPS - shift), at(shift)) for shift in (2, -2)]
    direct = [push(feats, group(band, HOPS - shift), at(shift)) for shift in (far, flip)]
    came_mine = [send_tile(other * 2 + b) for b in range(2)]

    ends, upto = [], jnp.int32(0)
    for g in range(graphs):
        upto = upto + sizes[g]
        ends.append(upto)

    def graph_of(spots):
        found = jnp.zeros(spots.shape, jnp.int32)
        for end in ends:
            found = found + (spots >= end).astype(jnp.int32)
        return found

    down = lax.broadcasted_iota(jnp.int32, (128, 128), 0)
    along = lax.broadcasted_iota(jnp.int32, (8, 128), 1)
    mine = [rep * 2, rep * 2 + 1]
    theirs = [other * 2, other * 2 + 1]

    def mask(j, b):
        row_ids = graph_of(down + (row * 4 + b) * 128)
        for k in range(4):
            ids = graph_of(along + cols_s[j, b, k] * 128)[:1, :]
            value = jnp.where(row_ids == ids, raw[j, b, k].astype(F32), 0.0).astype(BF16)
            masked[b, pl.ds(pl.multiple_of(j * 512 + k * 128, 128), 128), :] = value.T

    ones = jnp.ones((1024, 128), BF16)

    def count(b):
        deg_v[b] = 1.0 + dot(masked[b], ones, (0, 0))

    def scale(p):
        pulled = dot(cots[p], w2_v[half, :], (1, 1))
        for i in range(2):
            b = p * 2 + i
            scaled = (pulled[i * 128:(i + 1) * 128, :] / jnp.tile(deg_v[b], (1, 2))).astype(BF16)
            value = dot(masked[b], scaled, (1, 0))
            terms[b, :128, :] = (value[:128, :] + scaled.astype(F32)).astype(BF16)
            terms[b, 128:, :] = value[128:, :].astype(BF16)

    def slot_of(b, n):
        return jnp.clip(lax.rem(cols_s[n // 4, b, n % 4] + 64 - (row - HOPS) * 4, 64), 0, 27)

    got_cols.wait()
    got_tiles.wait()
    for b in mine + theirs:
        mask(rep, b)
    came_cols.wait_recv()
    more_cols = pull(cols_v, cols_s.at[other])
    more_cols.wait()
    for copy in came_mine:
        copy.wait_send()
    came_theirs = [send_tile(mine[0]), send_tile(mine[1])]
    for i in range(2):
        came_mine[i].wait_recv()
        mask(other, mine[i])
        count(mine[i])
    passed = []
    for n, shift in enumerate((2, -2)):
        near[n].wait_recv()
        passed.append(push(group(band, HOPS - shift), group(band, HOPS - shift - flip), sibling))
    got_feats.wait()
    for copy in direct + passed:
        copy.wait_recv()
    def span(s, p):
        return firsts.at[pl.ds(s * 4 + p * 2, 2)]

    def offer(p):
        return [push(span(HOPS, p), span(HOPS - shift, p), at(shift)) for shift in (2, -2, far, flip)]

    def smooth(b):
        near_x = jnp.concatenate([band[slot_of(b, n)] for n in range(8)], axis=0)
        value = dot(masked[b], near_x, (0, 0)) + band[HOPS * 4 + b].astype(F32)
        firsts[HOPS * 4 + b] = (value / deg_v[b]).astype(BF16)

    def hide(s):
        x = firsts[s * 4:(s + 1) * 4] if isinstance(s, int) else firsts[pl.ds(s * 4, 4)]
        value = jnp.maximum(dot(x.reshape(512, 128), w1_v[...], (1, 0)), 0.0).astype(BF16)
        hidden[pl.ds(s * 4, 4)] = value.reshape(4, 128, 256)

    for b in mine:
        smooth(b)
    waves = [offer(rep)]
    for copy in came_theirs:
        copy.wait_send()
    came_cot = push(cot, cots.at[rep], mate)
    for i in range(2):
        came_theirs[i].wait_recv()
        mask(other, theirs[i])
        count(theirs[i])
        smooth(theirs[i])
    waves.append(offer(other))
    got_cot.wait()
    got_w2.wait()
    got_w1.wait()
    scale(rep)
    hide(HOPS)
    handed = []
    for p, wave in zip((rep, other), waves):
        for n, shift in enumerate((2, -2)):
            wave[n].wait_recv()
            handed.append(push(span(HOPS - shift, p), span(HOPS - shift - flip, p), sibling))
    for wave in waves:
        wave[2].wait_recv()
        wave[3].wait_recv()
    for s in (HOPS + flip, HOPS - 2, HOPS + 2, HOPS + far):
        hide(s)
    came_cot.wait_recv()
    scale(other)
    for copy in handed:
        copy.wait_recv()
    for shift in (2, -2):
        hide(HOPS - shift + flip)

    for b in range(4):
        near_h = jnp.concatenate([hidden[slot_of(b, n)] for n in range(8)], axis=0)
        value = (dot(masked[b], near_h, (0, 0)) + hidden[HOPS * 4 + b].astype(F32)) / jnp.tile(deg_v[b], (1, 2))
        second_s[b // 2, (b % 2) * 128:(b % 2 + 1) * 128, :] = value.astype(BF16)
        near_f = jnp.concatenate([firsts[slot_of(b, n)] for n in range(8)], axis=0)
        value = dot(near_f, jnp.where(near_h > 0, terms[b], jnp.zeros_like(near_h)), (0, 0))
        gi = value if b == 0 else gi + value
    came_second = push(second_s.at[other], second_in, mate)
    for s in range(16):
        j, q = s // 8, s % 8
        part[s // 8, s % 8, 64:, :] = gi[q * 16:(q + 1) * 16, j * 128:(j + 1) * 128]

    def outer(c):
        lanes = pl.ds(pl.multiple_of(c * 256, 256), 256)
        go = dot(second_s[...].reshape(512, 256), cots[:, :, lanes].reshape(512, 256), (0, 0))
        for s in range(8):
            j, q = s // 4, s % 4
            part[c, s, :64, :] = go[q * 64:(q + 1) * 64, j * 128:(j + 1) * 128]

    outer(1 - core)
    joined = push(part.at[1 - core], paired, sibling)
    outer(core)
    joined.wait_recv()
    shares = []
    for q, peer in zip(order, peers):
        parcel[q] = (part[core, q] + paired[q]).astype(BF16)
        shares.append(push(parcel.at[q], parts.at[len(shares)], peer))
    total[...] = part[core, chip] + paired[chip]
    came_second.wait_recv()
    scores = dot(second_s[rep], w2_v[half, :], (1, 0))
    scores = scores + dot(second_in[...], w2_v[pl.ds(pl.multiple_of(other * 256, 256), 256), :], (1, 0))
    scores_o[...] = scores.astype(BF16)
    value = total[...]
    for t, copy in enumerate(shares):
        copy.wait_recv()
        value = value + parts[t].astype(F32)
    whole[rep, core, chip] = value.astype(BF16)

    def spread(p, c, q, peer):
        return push(whole.at[p, c, q], whole.at[p, c, q], peer)

    rounds = [spread(rep, core, chip, peer) for peer in peers[::-1]][::-1]
    beyond = [spread(rep, core, chip, mate)]
    aside = [spread(rep, core, chip, sibling)]
    for t, copy in enumerate(rounds):
        copy.wait_recv()
        beyond.append(spread(rep, core, order[t], mate))
        aside.append(spread(rep, core, order[t], sibling))
    for t, copy in enumerate(beyond):
        copy.wait_recv()
        aside.append(spread(other, core, chip if t == 0 else order[t - 1], sibling))
    for copy in aside:
        copy.wait_recv()
    for flight in flights:
        flight.wait_send()


def end_kernel(scores, whole, scores_o, gi_o, go_o, gi_s, go_s, sem):
    copies = [pltpu.make_async_copy(scores, scores_o, sem.at[0])]
    copies[0].start()
    for p in range(2):
        for s in range(16):
            piece = whole[p, s // 8, s % 8].astype(F32)
            j, q = s // 4, s % 4
            go_s[p * 256 + q * 64:p * 256 + (q + 1) * 64, j * 128:(j + 1) * 128] = piece[:64]
            j, q = s // 8, s % 8
            gi_s[q * 16:(q + 1) * 16, p * 256 + j * 128:p * 256 + (j + 1) * 128] = piece[64:]
        rows = pl.ds(p * 256, 256)
        copies.append(pltpu.make_async_copy(go_s.at[rows], go_o.at[rows], sem.at[1 + p]))
        copies[-1].start()
    copies.append(pltpu.make_async_copy(gi_s, gi_o, sem.at[3]))
    copies[-1].start()
    for copy in copies:
        copy.wait()


def fused(features, input_weight, output_weight, cotangent, adjacency_tiles, block_columns, graph_sizes):
    scores, whole = pl.pallas_call(
        fused_kernel,
        out_shape=(pltpu.VMEM((256, 512), BF16), pltpu.VMEM((2, 2, 8, 80, 128), BF16)),
        in_specs=[HBM, HBM, HBM, SMEM, HBM, HBM, HBM],
        out_specs=(VMEM,) * 2,
        scratch_shapes=[
            pltpu.VMEM((28, 128, 128), BF16),
            pltpu.VMEM((2, 4, 4, 128, 128), BF16),
            pltpu.VMEM((4, 1024, 128), BF16),
            pltpu.VMEM((2, 256, 512), BF16),
            pltpu.VMEM((128, 256), BF16),
            pltpu.VMEM((512, 512), BF16),
            pltpu.VMEM((4, 4), jnp.int32),
            pltpu.SMEM((2, 4, 4), jnp.int32),
            pltpu.VMEM((28, 128, 128), BF16),
            pltpu.VMEM((28, 128, 256), BF16),
            pltpu.VMEM((4, 1024, 256), BF16),
            pltpu.VMEM((4, 128, 128), F32),
            pltpu.VMEM((2, 256, 256), BF16),
            pltpu.VMEM((256, 256), BF16),
            pltpu.VMEM((2, 8, 80, 128), F32),
            pltpu.VMEM((8, 80, 128), F32),
            pltpu.VMEM((80, 128), F32),
            pltpu.VMEM((8, 80, 128), BF16),
            pltpu.VMEM((7, 80, 128), BF16),
            pltpu.SemaphoreType.DMA((72,)),
            pltpu.SemaphoreType.DMA((72,)),
            pltpu.SemaphoreType.DMA((8,)),
        ],
        compiler_params=pltpu.CompilerParams(vmem_limit_bytes=58 << 20, collective_id=0, has_side_effects=True),
    )(features.reshape(4, 128, 128), adjacency_tiles, block_columns, graph_sizes, input_weight, output_weight,
      cotangent)
    return pl.pallas_call(
        end_kernel,
        out_shape=(shape((256, 512), BF16), shape((128, 512), F32), shape((512, 512), F32)),
        in_specs=[VMEM] * 2,
        out_specs=(HBM,) * 3,
        scratch_shapes=[pltpu.VMEM((128, 512), F32), pltpu.VMEM((512, 512), F32), pltpu.SemaphoreType.DMA((4,))],
        compiler_params=params(),
    )(scores, whole)


def params(number=None):
    limit = 48 << 20
    if number is None:
        return pltpu.CompilerParams(vmem_limit_bytes=limit)
    return pltpu.CompilerParams(vmem_limit_bytes=limit, collective_id=number, has_side_effects=True)


def shape(dims, kind):
    return jax.ShapeDtypeStruct(dims, kind)


def sems(count):
    return [pltpu.SemaphoreType.DMA((count,)), pltpu.SemaphoreType.DMA((count,)), pltpu.SemaphoreType.DMA((4,))]


def body(
    features, input_weight, output_weight, cotangent, adjacency_tiles, block_columns, graph_sizes
):
    row = lax.axis_index("row")
    rows, reps = lax.axis_size("row"), lax.axis_size("rep")
    blocks, per, tile = adjacency_tiles.shape[:3]
    local = blocks * tile
    fin = features.shape[1]
    hid = output_weight.shape[0]
    half, quarter = hid // reps, local // reps
    nodes = rows * local
    if (rows, reps, blocks, per) == (16, 2, 4, 4) and graph_sizes.shape[0] <= 32:
        return fused(features, input_weight, output_weight, cotangent, adjacency_tiles, block_columns, graph_sizes)
    upto = jnp.arange(graph_sizes.shape[0])
    ends = jnp.sum(jnp.where(upto[None, :] <= upto[:, None], graph_sizes[None, :], 0), axis=1)

    def graph_of(places):
        return jnp.sum((places[..., None] >= ends).astype(jnp.int32), axis=-1)

    spots = lax.rem((row - HOPS) * local + nodes + jnp.arange(SPAN * local, dtype=jnp.int32), nodes)
    ids = graph_of(spots)
    row_ids = ids[HOPS * local:(HOPS + 1) * local].reshape(local, 1)
    band_ids = ids.reshape(SPAN * blocks, tile)
    padded = jnp.pad(block_columns, ((0, 8 - blocks), (0, 128 - per)))
    tall = hid * hid // reps // half + fin
    band, cots, all_tiles, all_cols = pl.pallas_call(
        functools.partial(open_kernel, rows, reps),
        out_shape=(
            shape((SPAN, local, fin), BF16),
            shape((reps, quarter, hid), BF16),
            shape((reps,) + adjacency_tiles.shape, BF16),
            shape((reps, 8, 128), jnp.int32),
        ),
        in_specs=[HBM] * 4,
        out_specs=(VMEM,) * 3 + (ANY,),
        scratch_shapes=sems(3 * (reps - 1) + 6),
        compiler_params=params(0),
    )(features, cotangent, adjacency_tiles, padded)
    dense, first, terms, own, degree = pl.pallas_call(
        functools.partial(full_front_kernel, rows, reps, blocks, tile),
        out_shape=(
            shape((local, SPAN * local), BF16),
            shape((local, fin), BF16),
            shape((SPAN, half, local), BF16),
            shape((local, half), F32),
            shape((local, 1), F32),
        ),
        in_specs=[VMEM, SMEM] + [VMEM] * 5,
        out_specs=(VMEM,) * 5,
        compiler_params=params(),
    )(all_tiles, all_cols, row_ids, band_ids, band, cots, output_weight)
    first_band, term_band = pl.pallas_call(
        functools.partial(band_kernel, rows),
        out_shape=(shape((SPAN, local, fin), BF16), shape((4, half, local), BF16)),
        in_specs=[VMEM] * 2,
        out_specs=(VMEM,) * 2,
        scratch_shapes=[pltpu.VMEM((2, half, local), BF16)] * 2 + sems(12),
        compiler_params=params(1),
    )(first, terms)
    second, grads = pl.pallas_call(
        functools.partial(back_kernel, reps),
        out_shape=(shape((local, half), BF16), shape((tall, half), F32)),
        in_specs=[VMEM] * 7,
        out_specs=(VMEM,) * 2,
        compiler_params=params(),
    )(dense, first_band, term_band, input_weight, own, degree, cots)
    second = second.reshape(reps, quarter, half)
    full = pl.pallas_call(
        functools.partial(swap_kernel, reps),
        out_shape=shape((reps, quarter, half), BF16),
        in_specs=[ANY],
        out_specs=ANY,
        scratch_shapes=sems(reps),
        compiler_params=params(2),
    )(second)
    whole = lax.all_gather(lax.psum(grads, "row"), "rep", axis=0)
    scores = dot(full.transpose(1, 0, 2).reshape(quarter, hid), output_weight, (1, 0)).astype(BF16)
    grad_input = whole[:, tall - fin:].transpose(1, 0, 2).reshape(fin, hid)
    grad_output = whole[:, :tall - fin].reshape(reps, hid // half, half, half)
    grad_output = grad_output.transpose(0, 2, 1, 3).reshape(hid, hid)
    return scores, grad_input, grad_output


def solution(mesh):
    placed = (
        P("row", None),
        P(),
        P(),
        P(("row", "rep"), None),
        P("row", "rep", None, None),
        P("row", "rep"),
        P(),
    )
    return jax.shard_map(
        body,
        mesh=mesh,
        in_specs=placed,
        out_specs=(P(("row", "rep"), None), P(), P()),
        check_vma=False,
    )
```

```python
import functools

import jax
import jax.numpy as jnp
from jax import lax
from jax.experimental import pallas as pl
from jax.experimental.pallas import tpu as pltpu
from jax.sharding import PartitionSpec as P

HOPS = 3
SPAN = 2 * HOPS + 1
MESH = pl.DeviceIdType.MESH
ANY = pl.BlockSpec(memory_space=pl.ANY)
HBM = pl.BlockSpec(memory_space=pltpu.HBM)
VMEM = pl.BlockSpec(memory_space=pltpu.VMEM)
SMEM = pl.BlockSpec(memory_space=pltpu.SMEM)
F32 = jnp.float32
BF16 = jnp.bfloat16


def dot(a, b, dims):
    return lax.dot_general(a, b, ((dims[:1], dims[1:]), ((), ())), preferred_element_type=F32)


def greet(peers):
    barrier = pltpu.get_barrier_semaphore()
    for peer in peers:
        pl.semaphore_signal(barrier, inc=1, device_id=peer, device_id_type=MESH)
    pl.semaphore_wait(barrier, len(peers))


def remote(src, dst, send, recv, index, peer):
    return pltpu.make_async_remote_copy(
        src_ref=src, dst_ref=dst, send_sem=send.at[index], recv_sem=recv.at[index],
        device_id=peer, device_id_type=MESH,
    )


def places(rows):
    row, rep = lax.axis_index("row"), lax.axis_index("rep")
    core = lax.rem(row, 2)
    flip, far = 1 - 2 * core, 6 * core - 3

    def at(shift):
        return (lax.rem(row + shift + rows, rows), rep)

    return flip, far, at


def start_rows(rows, src, band, send, recv, base):
    flip, far, at = places(rows)
    copies = [remote(src, band.at[HOPS - shift], send, recv, base + n, at(shift))
              for n, shift in enumerate((2, -2, far, flip))]
    for copy in copies:
        copy.start()
    return copies


def finish_rows(rows, copies, band, send, recv, base):
    flip, far, at = places(rows)
    passed = []
    for n, shift in enumerate((2, -2)):
        copies[n].wait_recv()
        step = remote(band.at[HOPS - shift], band.at[HOPS - shift - flip], send, recv, base + n, at(flip))
        step.start()
        passed.append(step)
    for copy in copies[2:]:
        copy.wait_recv()
    for copy in copies:
        copy.wait_send()
    for copy in passed:
        copy.wait()


def open_kernel(rows, reps, feats, cot, tiles, cols, band, cots, all_tiles, all_cols, send, recv, local):
    row, rep = lax.axis_index("row"), lax.axis_index("rep")
    flip, far, at = places(rows)
    others = [(row, lax.rem(rep + t, reps)) for t in range(1, reps)]
    greet([at(2), at(-2), at(far), at(flip)] + others)
    copies, n = [], 0
    pieces = ((tiles, all_tiles), (cols, all_cols), (cot, cots))
    pieces = pieces if cot is not None else pieces[:2]
    for peer in others:
        for src, dst in pieces:
            copies.append(remote(src, dst.at[rep], send, recv, n, peer))
            n += 1
    for i, (src, dst) in enumerate(pieces):
        copies.append(pltpu.make_async_copy(src, dst.at[rep], local.at[i]))
    copies.append(pltpu.make_async_copy(feats, band.at[HOPS], local.at[3]))
    for copy in copies:
        copy.start()
    moved = start_rows(rows, feats, band, send, recv, n)
    finish_rows(rows, moved, band, send, recv, n + 4)
    for copy in copies:
        copy.wait()


def scale_terms(rep, reps, cots, w2, dense, degree, terms):
    size = degree.shape[0]
    half = w2.shape[0] // reps
    at = pl.ds(pl.multiple_of(rep * half, half), half)
    pulled = dot(cots[...].reshape(size, -1), w2[at, :], (1, 1))
    scaled = (pulled / degree).astype(BF16)
    scaled_t = scaled.astype(F32).T.astype(BF16)
    for s in range(SPAN):
        part = dot(scaled_t, dense[:, s * size:(s + 1) * size], (1, 0))
        if s == HOPS:
            own = part.T + scaled.astype(F32)
        terms[s] = part.astype(BF16)
    return own


def front_kernel(rows, reps, blocks, tile, tiles, cols, row_ids, band_ids, band,
                 dense, first_o, deg_o):
    row = lax.axis_index("row")
    total = rows * blocks
    per = tiles.shape[2]
    dense[...] = jnp.zeros_like(dense)
    for b in range(blocks):
        at = pl.ds(b * tile, tile)
        ids = row_ids[at, :]
        sums = jnp.ones((tile, 1), F32)
        for j in range(reps):
            for k in range(per):
                slot = lax.rem(cols[j, b, k] + total - (row - HOPS) * blocks, total)
                same = ids == band_ids[pl.ds(slot, 1), :]
                value = jnp.where(same, tiles[j, b, k].astype(F32), 0.0)
                sums = sums + jnp.sum(value, axis=1, keepdims=True)
                dense[at, pl.ds(pl.multiple_of(slot * tile, tile), tile)] = value.astype(BF16)
        deg_o[at, :] = sums
    degree = deg_o[...]
    local = blocks * tile
    flat = band[...].reshape(SPAN * local, -1)
    summed = dot(dense[...], flat, (1, 0))
    first = ((summed + band[HOPS].astype(F32)) / degree).astype(BF16)
    first_o[...] = first


def full_front_kernel(rows, reps, blocks, tile, tiles, cols, row_ids, band_ids, band, cots, w2,
                      dense, first_o, terms_o, own_o, deg_o):
    front_kernel(rows, reps, blocks, tile, tiles, cols, row_ids, band_ids, band, dense, first_o, deg_o)
    own_o[...] = scale_terms(lax.axis_index("rep"), reps, cots, w2, dense, deg_o[...], terms_o)


def band_kernel(rows, first, terms, first_band, term_band, pair, joint, send, recv, local):
    flip, far, at = places(rows)
    greet([at(2), at(-2), at(far), at(flip)])
    joined = [remote(terms.at[HOPS + shift + flip], pair.at[n], send, recv, n, at(flip))
              for n, shift in enumerate((2, -2))]
    for copy in joined:
        copy.start()
    direct = [remote(terms.at[HOPS + far], term_band.at[2], send, recv, 2, at(far))]
    direct[0].start()
    moved = start_rows(rows, first, first_band, send, recv, 3)
    keep = pltpu.make_async_copy(first, first_band.at[HOPS], local.at[0])
    keep.start()
    direct.append(remote(terms.at[HOPS + flip], term_band.at[3], send, recv, 7, at(flip)))
    direct[1].start()
    for n, shift in enumerate((2, -2)):
        joined[n].wait_recv()
        joint[n] = (terms[HOPS + shift].astype(F32) + pair[n].astype(F32)).astype(BF16)
        step = remote(joint.at[n], term_band.at[n], send, recv, 8 + n, at(shift))
        step.start()
        direct.append(step)
    finish_rows(rows, moved, first_band, send, recv, 10)
    keep.wait()
    for copy in joined:
        copy.wait_send()
    for copy in direct:
        copy.wait()


def back_kernel(reps, dense, first_band, term_band, w1, own, deg, cots, second_o, grads_o):
    rep = lax.axis_index("rep")
    local, half = own.shape
    weight = w1[:, pl.ds(pl.multiple_of(rep * half, half), half)]
    preact = dot(first_band[HOPS], weight, (1, 0))
    mine = jnp.maximum(preact, 0.0).astype(BF16)
    summed = mine.astype(F32)
    for s in range(SPAN):
        hidden = mine if s == HOPS else jnp.maximum(dot(first_band[s], weight, (1, 0)), 0.0).astype(BF16)
        summed = summed + dot(dense[:, s * local:(s + 1) * local], hidden, (1, 0))
    second = (summed / deg[...]).astype(BF16)
    second_o[...] = second
    out = dot(second, cots[...].reshape(local, -1), (0, 0))
    width = out.shape[1] // half
    for i in range(width):
        grads_o[i * half:(i + 1) * half, :] = out[:, i * half:(i + 1) * half]
    got = term_band[0].astype(F32)
    for i in range(1, 4):
        got = got + term_band[i].astype(F32)
    back = got.T + own[...]
    delta = jnp.where(preact > 0.0, back, 0.0).astype(BF16)
    grads_o[width * half:, :] = dot(first_band[HOPS], delta, (0, 0))


def swap_kernel(reps, second, full, send, recv, local):
    row, rep = lax.axis_index("row"), lax.axis_index("rep")
    others = [(row, lax.rem(rep + t, reps)) for t in range(1, reps)]
    greet(others)
    copies = [remote(second.at[peer[1]], full.at[rep], send, recv, n, peer) for n, peer in enumerate(others)]
    copies.append(pltpu.make_async_copy(second.at[rep], full.at[rep], local.at[0]))
    for copy in copies:
        copy.start()
    for copy in copies:
        copy.wait()


class Flight:
    def __init__(self, copy):
        self.copy, self.landed, self.left = copy, False, False
        copy.start()

    def wait_send(self):
        if not self.left:
            self.copy.wait_send()
        self.left = True

    def wait_recv(self):
        if not self.landed:
            self.copy.wait_recv()
        self.landed = True

    def wait(self):
        if not self.landed:
            self.copy.wait()
        self.landed = True


def fused_kernel(feats, tiles, cols, sizes, w1, w2, cot, scores_o, whole,
                 band, raw, masked, cots, w1_v, w2_v, cols_v, cols_s, firsts, hidden, terms, deg_v,
                 second_s, second_in, part, paired, total, parcel, parts, send, recv, local):
    row, rep = lax.axis_index("row"), lax.axis_index("rep")
    graphs = sizes.shape[0]
    chip, core = row // 2, lax.rem(row, 2)
    other = 1 - rep
    flip, far, at = places(16)
    mate, sibling = (row, other), at(flip)
    deep, mid, low = chip // 4, lax.rem(chip // 2, 2), lax.rem(chip, 2)
    peers, order = [], []
    for m in range(1, 8):
        q = lax.rem(deep + m // 4, 2) * 4 + lax.rem(mid + m // 2 % 2, 2) * 2 + lax.rem(low + m % 2, 2)
        order.append(q)
        peers.append((q * 2 + core, rep))
    flights, pulls = [], []

    def push(src, dst, peer):
        flights.append(Flight(remote(src, dst, send, recv, len(flights), peer)))
        return flights[-1]

    def pull(src, dst):
        pulls.append(Flight(pltpu.make_async_copy(src, dst, local.at[len(pulls)])))
        return pulls[-1]

    half = pl.ds(pl.multiple_of(rep * 256, 256), 256)
    got_cols = pull(cols, cols_s.at[rep])
    got_tiles = pull(tiles, raw.at[rep])
    got_cot = pull(cot, cots.at[rep])
    got_w2 = pull(w2, w2_v)
    got_w1 = pull(w1.at[:, half], w1_v)
    got_feats = pull(feats, band.at[pl.ds(HOPS * 4, 4)])

    def send_tile(b):
        return push(tiles.at[b], raw.at[rep, b], mate)

    def group(ref, s):
        return ref.at[pl.ds(s * 4, 4)]

    greet(peers[::-1] + [at(far), mate, sibling])
    came_cols = push(cols, cols_v, mate)
    near = [push(feats, group(band, HOPS - shift), at(shift)) for shift in (2, -2)]
    direct = [push(feats, group(band, HOPS - shift), at(shift)) for shift in (far, flip)]
    came_mine = [send_tile(other * 2 + b) for b in range(2)]

    ends, upto = [], jnp.int32(0)
    for g in range(graphs):
        upto = upto + sizes[g]
        ends.append(upto)

    def graph_of(spots):
        found = jnp.zeros(spots.shape, jnp.int32)
        for end in ends:
            found = found + (spots >= end).astype(jnp.int32)
        return found

    down = lax.broadcasted_iota(jnp.int32, (128, 128), 0)
    along = lax.broadcasted_iota(jnp.int32, (8, 128), 1)
    mine = [rep * 2, rep * 2 + 1]
    theirs = [other * 2, other * 2 + 1]

    def mask(j, b):
        row_ids = graph_of(down + (row * 4 + b) * 128)
        for k in range(4):
            ids = graph_of(along + cols_s[j, b, k] * 128)[:1, :]
            value = jnp.where(row_ids == ids, raw[j, b, k].astype(F32), 0.0).astype(BF16)
            masked[b, pl.ds(pl.multiple_of(j * 512 + k * 128, 128), 128), :] = value.T

    ones = jnp.ones((1024, 128), BF16)

    def count(b):
        deg_v[b] = 1.0 + dot(masked[b], ones, (0, 0))

    def scale(p):
        pulled = dot(cots[p], w2_v[half, :], (1, 1))
        for i in range(2):
            b = p * 2 + i
            scaled = (pulled[i * 128:(i + 1) * 128, :] / jnp.tile(deg_v[b], (1, 2))).astype(BF16)
            value = dot(masked[b], scaled, (1, 0))
            terms[b, :128, :] = (value[:128, :] + scaled.astype(F32)).astype(BF16)
            terms[b, 128:, :] = value[128:, :].astype(BF16)

    def slot_of(b, n):
        return jnp.clip(lax.rem(cols_s[n // 4, b, n % 4] + 64 - (row - HOPS) * 4, 64), 0, 27)

    got_cols.wait()
    got_tiles.wait()
    for b in mine + theirs:
        mask(rep, b)
    came_cols.wait_recv()
    more_cols = pull(cols_v, cols_s.at[other])
    more_cols.wait()
    for copy in came_mine:
        copy.wait_send()
    came_theirs = [send_tile(mine[0]), send_tile(mine[1])]
    passed = []
    for n, shift in enumerate((2, -2)):
        copies[n].wait_recv()
        step = remote(band.at[HOPS - shift], band.at[HOPS - shift - flip], send, recv, base + n, at(flip))
        step.start()
        passed.append(step)
    for copy in copies[2:]:
        copy.wait_recv()
    for copy in copies:
        copy.wait_send()
    for copy in passed:
        copy.wait()


def open_kernel(rows, reps, feats, cot, tiles, cols, band, cots, all_tiles, all_cols, send, recv, local):
    row, rep = lax.axis_index("row"), lax.axis_index("rep")
    flip, far, at = places(rows)
    others = [(row, lax.rem(rep + t, reps)) for t in range(1, reps)]
    greet([at(2), at(-2), at(far), at(flip)] + others)
    copies, n = [], 0
    pieces = ((tiles, all_tiles), (cols, all_cols), (cot, cots))
    pieces = pieces if cot is not None else pieces[:2]
    for peer in others:
        for src, dst in pieces:
            copies.append(remote(src, dst.at[rep], send, recv, n, peer))
            n += 1
    for i, (src, dst) in enumerate(pieces):
        copies.append(pltpu.make_async_copy(src, dst.at[rep], local.at[i]))
    copies.append(pltpu.make_async_copy(feats, band.at[HOPS], local.at[3]))
    for copy in copies:
        copy.start()
    moved = start_rows(rows, feats, band, send, recv, n)
    finish_rows(rows, moved, band, send, recv, n + 4)
    for copy in copies:
        copy.wait()


def scale_terms(rep, reps, cots, w2, dense, degree, terms):
    size = degree.shape[0]
    half = w2.shape[0] // reps
    at = pl.ds(pl.multiple_of(rep * half, half), half)
    pulled = dot(cots[...].reshape(size, -1), w2[at, :], (1, 1))
    scaled = (pulled / degree).astype(BF16)
    scaled_t = scaled.astype(F32).T.astype(BF16)
    for s in range(SPAN):
        part = dot(scaled_t, dense[:, s * size:(s + 1) * size], (1, 0))
        if s == HOPS:
            own = part.T + scaled.astype(F32)
        terms[s] = part.astype(BF16)
    return own


def front_kernel(rows, reps, blocks, tile, tiles, cols, row_ids, band_ids, band,
                 dense, first_o, deg_o):
    row = lax.axis_index("row")
    total = rows * blocks
    per = tiles.shape[2]
    dense[...] = jnp.zeros_like(dense)
    for b in range(blocks):
        at = pl.ds(b * tile, tile)
        ids = row_ids[at, :]
        sums = jnp.ones((tile, 1), F32)
        for j in range(reps):
            for k in range(per):
                slot = lax.rem(cols[j, b, k] + total - (row - HOPS) * blocks, total)
                same = ids == band_ids[pl.ds(slot, 1), :]
                value = jnp.where(same, tiles[j, b, k].astype(F32), 0.0)
                sums = sums + jnp.sum(value, axis=1, keepdims=True)
                dense[at, pl.ds(pl.multiple_of(slot * tile, tile), tile)] = value.astype(BF16)
        deg_o[at, :] = sums
    degree = deg_o[...]
    local = blocks * tile
    flat = band[...].reshape(SPAN * local, -1)
    summed = dot(dense[...], flat, (1, 0))
    first = ((summed + band[HOPS].astype(F32)) / degree).astype(BF16)
    first_o[...] = first


def full_front_kernel(rows, reps, blocks, tile, tiles, cols, row_ids, band_ids, band, cots, w2,
                      dense, first_o, terms_o, own_o, deg_o):
    front_kernel(rows, reps, blocks, tile, tiles, cols, row_ids, band_ids, band, dense, first_o, deg_o)
    own_o[...] = scale_terms(lax.axis_index("rep"), reps, cots, w2, dense, deg_o[...], terms_o)


def band_kernel(rows, first, terms, first_band, term_band, pair, joint, send, recv, local):
    flip, far, at = places(rows)
    greet([at(2), at(-2), at(far), at(flip)])
    joined = [remote(terms.at[HOPS + shift + flip], pair.at[n], send, recv, n, at(flip))
              for n, shift in enumerate((2, -2))]
    for copy in joined:
        copy.start()
    direct = [remote(terms.at[HOPS + far], term_band.at[2], send, recv, 2, at(far))]
    direct[0].start()
    moved = start_rows(rows, first, first_band, send, recv, 3)
    keep = pltpu.make_async_copy(first, first_band.at[HOPS], local.at[0])
    keep.start()
    direct.append(remote(terms.at[HOPS + flip], term_band.at[3], send, recv, 7, at(flip)))
    direct[1].start()
    for n, shift in enumerate((2, -2)):
        joined[n].wait_recv()
        joint[n] = (terms[HOPS + shift].astype(F32) + pair[n].astype(F32)).astype(BF16)
        step = remote(joint.at[n], term_band.at[n], send, recv, 8 + n, at(shift))
        step.start()
        direct.append(step)
    finish_rows(rows, moved, first_band, send, recv, 10)
    keep.wait()
    for copy in joined:
        copy.wait_send()
    for copy in direct:
        copy.wait()


def back_kernel(reps, dense, first_band, term_band, w1, own, deg, cots, second_o, grads_o):
    rep = lax.axis_index("rep")
    local, half = own.shape
    weight = w1[:, pl.ds(pl.multiple_of(rep * half, half), half)]
    preact = dot(first_band[HOPS], weight, (1, 0))
    mine = jnp.maximum(preact, 0.0).astype(BF16)
    summed = mine.astype(F32)
    for s in range(SPAN):
        hidden = mine if s == HOPS else jnp.maximum(dot(first_band[s], weight, (1, 0)), 0.0).astype(BF16)
        summed = summed + dot(dense[:, s * local:(s + 1) * local], hidden, (1, 0))
    second = (summed / deg[...]).astype(BF16)
    second_o[...] = second
    out = dot(second, cots[...].reshape(local, -1), (0, 0))
    width = out.shape[1] // half
    for i in range(width):
        grads_o[i * half:(i + 1) * half, :] = out[:, i * half:(i + 1) * half]
    got = term_band[0].astype(F32)
    for i in range(1, 4):
        got = got + term_band[i].astype(F32)
    back = got.T + own[...]
    delta = jnp.where(preact > 0.0, back, 0.0).astype(BF16)
    grads_o[width * half:, :] = dot(first_band[HOPS], delta, (0, 0))


def swap_kernel(reps, second, full, send, recv, local):
    row, rep = lax.axis_index("row"), lax.axis_index("rep")
    others = [(row, lax.rem(rep + t, reps)) for t in range(1, reps)]
    greet(others)
    copies = [remote(second.at[peer[1]], full.at[rep], send, recv, n, peer) for n, peer in enumerate(others)]
    copies.append(pltpu.make_async_copy(second.at[rep], full.at[rep], local.at[0]))
    for copy in copies:
        copy.start()
    for copy in copies:
        copy.wait()


class Flight:
    def __init__(self, copy):
        self.copy, self.landed, self.left = copy, False, False
        copy.start()

    def wait_send(self):
        if not self.left:
            self.copy.wait_send()
        self.left = True

    def wait_recv(self):
        if not self.landed:
            self.copy.wait_recv()
        self.landed = True

    def wait(self):
        if not self.landed:
            self.copy.wait()
        self.landed = True


def fused_kernel(feats, tiles, cols, sizes, w1, w2, cot, scores_o, whole,
                 band, raw, masked, cots, w1_v, w2_v, cols_v, cols_s, firsts, hidden, terms, deg_v,
                 second_s, second_in, part, paired, total, parcel, parts, send, recv, local):
    row, rep = lax.axis_index("row"), lax.axis_index("rep")
    graphs = sizes.shape[0]
    chip, core = row // 2, lax.rem(row, 2)
    other = 1 - rep
    flip, far, at = places(16)
    mate, sibling = (row, other), at(flip)
    deep, mid, low = chip // 4, lax.rem(chip // 2, 2), lax.rem(chip, 2)
    peers, order = [], []
    for m in range(1, 8):
        q = lax.rem(deep + m // 4, 2) * 4 + lax.rem(mid + m // 2 % 2, 2) * 2 + lax.rem(low + m % 2, 2)
        order.append(q)
        peers.append((q * 2 + core, rep))
    flights, pulls = [], []

    def push(src, dst, peer):
        flights.append(Flight(remote(src, dst, send, recv, len(flights), peer)))
        return flights[-1]

    def pull(src, dst):
        pulls.append(Flight(pltpu.make_async_copy(src, dst, local.at[len(pulls)])))
        return pulls[-1]

    half = pl.ds(pl.multiple_of(rep * 256, 256), 256)
    got_cols = pull(cols, cols_s.at[rep])
    got_tiles = pull(tiles, raw.at[rep])
    got_cot = pull(cot, cots.at[rep])
    got_w2 = pull(w2, w2_v)
    got_w1 = pull(w1.at[:, half], w1_v)
    got_feats = pull(feats, band.at[pl.ds(HOPS * 4, 4)])

    def send_tile(b):
        return push(tiles.at[b], raw.at[rep, b], mate)

    def group(ref, s):
        return ref.at[pl.ds(s * 4, 4)]

    greet(peers[::-1] + [at(far), mate, sibling])
    came_cols = push(cols, cols_v, mate)
    near = [push(feats, group(band, HOPS - shift), at(shift)) for shift in (2, -2)]
    direct = [push(feats, group(band, HOPS - shift), at(shift)) for shift in (far, flip)]
    came_mine = [send_tile(other * 2 + b) for b in range(2)]

    ends, upto = [], jnp.int32(0)
    for g in range(graphs):
        upto = upto + sizes[g]
        ends.append(upto)

    def graph_of(spots):
        found = jnp.zeros(spots.shape, jnp.int32)
        for end in ends:
            found = found + (spots >= end).astype(jnp.int32)
        return found

    down = lax.broadcasted_iota(jnp.int32, (128, 128), 0)
    along = lax.broadcasted_iota(jnp.int32, (8, 128), 1)
    mine = [rep * 2, rep * 2 + 1]
    theirs = [other * 2, other * 2 + 1]

    def mask(j, b):
        row_ids = graph_of(down + (row * 4 + b) * 128)
        for k in range(4):
            ids = graph_of(along + cols_s[j, b, k] * 128)[:1, :]
            value = jnp.where(row_ids == ids, raw[j, b, k].astype(F32), 0.0).astype(BF16)
            masked[b, pl.ds(pl.multiple_of(j * 512 + k * 128, 128), 128), :] = value.T

    ones = jnp.ones((1024, 128), BF16)

    def count(b):
        deg_v[b] = 1.0 + dot(masked[b], ones, (0, 0))

    def scale(p):
        pulled = dot(cots[p], w2_v[half, :], (1, 1))
        for i in range(2):
            b = p * 2 + i
            scaled = (pulled[i * 128:(i + 1) * 128, :] / jnp.tile(deg_v[b], (1, 2))).astype(BF16)
            value = dot(masked[b], scaled, (1, 0))
            terms[b, :128, :] = (value[:128, :] + scaled.astype(F32)).astype(BF16)
            terms[b, 128:, :] = value[128:, :].astype(BF16)

    def slot_of(b, n):
        return jnp.clip(lax.rem(cols_s[n // 4, b, n % 4] + 64 - (row - HOPS) * 4, 64), 0, 27)

    got_cols.wait()
    got_tiles.wait()
    for b in mine + theirs:
        mask(rep, b)
    came_cols.wait_recv()
    more_cols = pull(cols_v, cols_s.at[other])
    more_cols.wait()
    for copy in came_mine:
        copy.wait_send()
    came_theirs = [send_tile(mine[0]), send_tile(mine[1])]
    for i in range(2):
        came_mine[i].wait_recv()
        mask(other, mine[i])
        count(mine[i])
    passed = []
    for n, shift in enumerate((2, -2)):
        near[n].wait_recv()
        passed.append(push(group(band, HOPS - shift), group(band, HOPS - shift - flip), sibling))
    got_feats.wait()
    for copy in direct + passed:
        copy.wait_recv()
    def span(s, p):
        return firsts.at[pl.ds(s * 4 + p * 2, 2)]

    def offer(p):
        return [push(span(HOPS, p), span(HOPS - shift, p), at(shift)) for shift in (2, -2, far, flip)]

    def smooth(b):
        near_x = jnp.concatenate([band[slot_of(b, n)] for n in range(8)], axis=0)
        value = dot(masked[b], near_x, (0, 0)) + band[HOPS * 4 + b].astype(F32)
        firsts[HOPS * 4 + b] = (value / deg_v[b]).astype(BF16)

    def hide(s):
        x = firsts[s * 4:(s + 1) * 4] if isinstance(s, int) else firsts[pl.ds(s * 4, 4)]
        value = jnp.maximum(dot(x.reshape(512, 128), w1_v[...], (1, 0)), 0.0).astype(BF16)
        hidden[pl.ds(s * 4, 4)] = value.reshape(4, 128, 256)

    for b in mine:
        smooth(b)
    waves = [offer(rep)]
    for copy in came_theirs:
        copy.wait_send()
    came_cot = push(cot, cots.at[rep], mate)
    for i in range(2):
        came_theirs[i].wait_recv()
        mask(other, theirs[i])
        count(theirs[i])
        smooth(theirs[i])
    waves.append(offer(other))
    got_cot.wait()
    got_w2.wait()
    got_w1.wait()
    scale(rep)
    hide(HOPS)
    handed = []
    for p, wave in zip((rep, other), waves):
        for n, shift in enumerate((2, -2)):
            wave[n].wait_recv()
            handed.append(push(span(HOPS - shift, p), span(HOPS - shift - flip, p), sibling))
    for wave in waves:
        wave[2].wait_recv()
        wave[3].wait_recv()
    for s in (HOPS + flip, HOPS - 2, HOPS + 2, HOPS + far):
        hide(s)
    came_cot.wait_recv()
    scale(other)
    for copy in handed:
        copy.wait_recv()
    for shift in (2, -2):
        hide(HOPS - shift + flip)

    for b in range(4):
        near_h = jnp.concatenate([hidden[slot_of(b, n)] for n in range(8)], axis=0)
        value = (dot(masked[b], near_h, (0, 0)) + hidden[HOPS * 4 + b].astype(F32)) / jnp.tile(deg_v[b], (1, 2))
        second_s[b // 2, (b % 2) * 128:(b % 2 + 1) * 128, :] = value.astype(BF16)
        near_f = jnp.concatenate([firsts[slot_of(b, n)] for n in range(8)], axis=0)
        value = dot(near_f, jnp.where(near_h > 0, terms[b], jnp.zeros_like(near_h)), (0, 0))
        gi = value if b == 0 else gi + value
    came_second = push(second_s.at[other], second_in, mate)
    for s in range(16):
        j, q = s // 8, s % 8
        part[s // 8, s % 8, 64:, :] = gi[q * 16:(q + 1) * 16, j * 128:(j + 1) * 128]

    def outer(c):
        lanes = pl.ds(pl.multiple_of(c * 256, 256), 256)
        go = dot(second_s[...].reshape(512, 256), cots[:, :, lanes].reshape(512, 256), (0, 0))
        for s in range(8):
            j, q = s // 4, s % 4
            part[c, s, :64, :] = go[q * 64:(q + 1) * 64, j * 128:(j + 1) * 128]

    outer(1 - core)
    joined = push(part.at[1 - core], paired, sibling)
    outer(core)
    joined.wait_recv()
    shares = []
    for q, peer in zip(order, peers):
        parcel[q] = (part[core, q] + paired[q]).astype(BF16)
        shares.append(push(parcel.at[q], parts.at[len(shares)], peer))
    total[...] = part[core, chip] + paired[chip]
    came_second.wait_recv()
    scores = dot(second_s[rep], w2_v[half, :], (1, 0))
    scores = scores + dot(second_in[...], w2_v[pl.ds(pl.multiple_of(other * 256, 256), 256), :], (1, 0))
    scores_o[...] = scores.astype(BF16)
    value = total[...]
    for t, copy in enumerate(shares):
        copy.wait_recv()
        value = value + parts[t].astype(F32)
    whole[rep, core, chip] = value.astype(BF16)

    def spread(p, c, q, peer):
        return push(whole.at[p, c, q], whole.at[p, c, q], peer)

    rounds = [spread(rep, core, chip, peer) for peer in peers[::-1]][::-1]
    beyond = [spread(rep, core, chip, mate)]
    aside = [spread(rep, core, chip, sibling)]
    for t, copy in enumerate(rounds):
        copy.wait_recv()
        beyond.append(spread(rep, core, order[t], mate))
        aside.append(spread(rep, core, order[t], sibling))
    for t, copy in enumerate(beyond):
        copy.wait_recv()
        aside.append(spread(other, core, chip if t == 0 else order[t - 1], sibling))
    for copy in aside:
        copy.wait_recv()
    for flight in flights:
        flight.wait_send()


def end_kernel(scores, whole, scores_o, gi_o, go_o, gi_s, go_s, sem):
    copies = [pltpu.make_async_copy(scores, scores_o, sem.at[0])]
    copies[0].start()
    for p in range(2):
        for s in range(16):
            piece = whole[p, s // 8, s % 8].astype(F32)
            j, q = s // 4, s % 4
            go_s[p * 256 + q * 64:p * 256 + (q + 1) * 64, j * 128:(j + 1) * 128] = piece[:64]
            j, q = s // 8, s % 8
            gi_s[q * 16:(q + 1) * 16, p * 256 + j * 128:p * 256 + (j + 1) * 128] = piece[64:]
        rows = pl.ds(p * 256, 256)
        copies.append(pltpu.make_async_copy(go_s.at[rows], go_o.at[rows], sem.at[1 + p]))
        copies[-1].start()
    copies.append(pltpu.make_async_copy(gi_s, gi_o, sem.at[3]))
    copies[-1].start()
    for copy in copies:
        copy.wait()


def fused(features, input_weight, output_weight, cotangent, adjacency_tiles, block_columns, graph_sizes):
    scores, whole = pl.pallas_call(
        fused_kernel,
        out_shape=(pltpu.VMEM((256, 512), BF16), pltpu.VMEM((2, 2, 8, 80, 128), BF16)),
        in_specs=[HBM, HBM, HBM, SMEM, HBM, HBM, HBM],
        out_specs=(VMEM,) * 2,
        scratch_shapes=[
            pltpu.VMEM((28, 128, 128), BF16),
            pltpu.VMEM((2, 4, 4, 128, 128), BF16),
            pltpu.VMEM((4, 1024, 128), BF16),
            pltpu.VMEM((2, 256, 512), BF16),
            pltpu.VMEM((128, 256), BF16),
            pltpu.VMEM((512, 512), BF16),
            pltpu.VMEM((4, 4), jnp.int32),
            pltpu.SMEM((2, 4, 4), jnp.int32),
            pltpu.VMEM((28, 128, 128), BF16),
            pltpu.VMEM((28, 128, 256), BF16),
            pltpu.VMEM((4, 1024, 256), BF16),
            pltpu.VMEM((4, 128, 128), F32),
            pltpu.VMEM((2, 256, 256), BF16),
            pltpu.VMEM((256, 256), BF16),
            pltpu.VMEM((2, 8, 80, 128), F32),
            pltpu.VMEM((8, 80, 128), F32),
            pltpu.VMEM((80, 128), F32),
            pltpu.VMEM((8, 80, 128), BF16),
            pltpu.VMEM((7, 80, 128), BF16),
            pltpu.SemaphoreType.DMA((72,)),
            pltpu.SemaphoreType.DMA((72,)),
            pltpu.SemaphoreType.DMA((8,)),
        ],
        compiler_params=pltpu.CompilerParams(vmem_limit_bytes=58 << 20, collective_id=0, has_side_effects=True),
    )(features.reshape(4, 128, 128), adjacency_tiles, block_columns, graph_sizes, input_weight, output_weight,
      cotangent)
    return pl.pallas_call(
        end_kernel,
        out_shape=(shape((256, 512), BF16), shape((128, 512), F32), shape((512, 512), F32)),
        in_specs=[VMEM] * 2,
        out_specs=(HBM,) * 3,
        scratch_shapes=[pltpu.VMEM((128, 512), F32), pltpu.VMEM((512, 512), F32), pltpu.SemaphoreType.DMA((4,))],
        compiler_params=params(),
    )(scores, whole)


def params(number=None):
    limit = 48 << 20
    if number is None:
        return pltpu.CompilerParams(vmem_limit_bytes=limit)
    return pltpu.CompilerParams(vmem_limit_bytes=limit, collective_id=number, has_side_effects=True)


def shape(dims, kind):
    return jax.ShapeDtypeStruct(dims, kind)


def sems(count):
    return [pltpu.SemaphoreType.DMA((count,)), pltpu.SemaphoreType.DMA((count,)), pltpu.SemaphoreType.DMA((4,))]


def body(
    features, input_weight, output_weight, cotangent, adjacency_tiles, block_columns, graph_sizes
):
    row = lax.axis_index("row")
    rows, reps = lax.axis_size("row"), lax.axis_size("rep")
    blocks, per, tile = adjacency_tiles.shape[:3]
    local = blocks * tile
    fin = features.shape[1]
    hid = output_weight.shape[0]
    half, quarter = hid // reps, local // reps
    nodes = rows * local
    if (rows, reps, blocks, per) == (16, 2, 4, 4) and graph_sizes.shape[0] <= 32:
        return fused(features, input_weight, output_weight, cotangent, adjacency_tiles, block_columns, graph_sizes)
    upto = jnp.arange(graph_sizes.shape[0])
    ends = jnp.sum(jnp.where(upto[None, :] <= upto[:, None], graph_sizes[None, :], 0), axis=1)

    def graph_of(places):
        return jnp.sum((places[..., None] >= ends).astype(jnp.int32), axis=-1)

    spots = lax.rem((row - HOPS) * local + nodes + jnp.arange(SPAN * local, dtype=jnp.int32), nodes)
    ids = graph_of(spots)
    row_ids = ids[HOPS * local:(HOPS + 1) * local].reshape(local, 1)
    band_ids = ids.reshape(SPAN * blocks, tile)
    padded = jnp.pad(block_columns, ((0, 8 - blocks), (0, 128 - per)))
    tall = hid * hid // reps // half + fin
    band, cots, all_tiles, all_cols = pl.pallas_call(
        functools.partial(open_kernel, rows, reps),
        out_shape=(
            shape((SPAN, local, fin), BF16),
            shape((reps, quarter, hid), BF16),
            shape((reps,) + adjacency_tiles.shape, BF16),
            shape((reps, 8, 128), jnp.int32),
        ),
        in_specs=[HBM] * 4,
        out_specs=(VMEM,) * 3 + (ANY,),
        scratch_shapes=sems(3 * (reps - 1) + 6),
        compiler_params=params(0),
    )(features, cotangent, adjacency_tiles, padded)
    dense, first, terms, own, degree = pl.pallas_call(
        functools.partial(full_front_kernel, rows, reps, blocks, tile),
        out_shape=(
            shape((local, SPAN * local), BF16),
            shape((local, fin), BF16),
            shape((SPAN, half, local), BF16),
            shape((local, half), F32),
            shape((local, 1), F32),
        ),
        in_specs=[VMEM, SMEM] + [VMEM] * 5,
        out_specs=(VMEM,) * 5,
        compiler_params=params(),
    )(all_tiles, all_cols, row_ids, band_ids, band, cots, output_weight)
    first_band, term_band = pl.pallas_call(
        functools.partial(band_kernel, rows),
        out_shape=(shape((SPAN, local, fin), BF16), shape((4, half, local), BF16)),
        in_specs=[VMEM] * 2,
        out_specs=(VMEM,) * 2,
        scratch_shapes=[pltpu.VMEM((2, half, local), BF16)] * 2 + sems(12),
        compiler_params=params(1),
    )(first, terms)
    second, grads = pl.pallas_call(
        functools.partial(back_kernel, reps),
        out_shape=(shape((local, half), BF16), shape((tall, half), F32)),
        in_specs=[VMEM] * 7,
        out_specs=(VMEM,) * 2,
        compiler_params=params(),
    )(dense, first_band, term_band, input_weight, own, degree, cots)
    second = second.reshape(reps, quarter, half)
    full = pl.pallas_call(
        functools.partial(swap_kernel, reps),
        out_shape=shape((reps, quarter, half), BF16),
        in_specs=[ANY],
        out_specs=ANY,
        scratch_shapes=sems(reps),
        compiler_params=params(2),
    )(second)
    whole = lax.all_gather(lax.psum(grads, "row"), "rep", axis=0)
    scores = dot(full.transpose(1, 0, 2).reshape(quarter, hid), output_weight, (1, 0)).astype(BF16)
    grad_input = whole[:, tall - fin:].transpose(1, 0, 2).reshape(fin, hid)
    grad_output = whole[:, :tall - fin].reshape(reps, hid // half, half, half)
    grad_output = grad_output.transpose(0, 2, 1, 3).reshape(hid, hid)
    return scores, grad_input, grad_output


def solution(mesh):
    placed = (
        P("row", None),
        P(),
        P(),
        P(("row", "rep"), None),
        P("row", "rep", None, None),
        P("row", "rep"),
        P(),
    )
    return jax.shard_map(
        body,
        mesh=mesh,
        in_specs=placed,
        out_specs=(P(("row", "rep"), None), P(), P()),
        check_vma=False,
    )
```
